1024 devices in a mesh: tensor: 4 (over x), shard: 32 (over z), replica: 8 (over y, core).
Axes of the slice: x: 4, y: 4, z: 32, core: 2. Of those that a mesh axis runs over, the one named last changes fastest.
Arguments:
- grad_parts: bfloat16 [8, 2, 16, 512, 4096], P('replica', None, 'tensor', None, 'shard'), may hold values from -6 to 6
- block_owner: int32 [2, 16, 8], P(None, 'tensor'), may hold values from 0 to 255, as said below
- left_stat: bfloat16 [4, 32, 1, 8, 512, 512], P('tensor', 'shard', None, 'replica'), as said below
- right_stat: bfloat16 [4, 32, 1, 8, 512, 512], P('tensor', 'shard', None, 'replica'), as said below
Outputs:
- shampoo_update: bfloat16 [2, 16, 512, 4096], P(None, 'tensor', 'replica', 'shard')
- block_rms: float32 [4, 32, 1, 8], P('tensor', 'shard', None, 'replica')
- left_next: bfloat16 [4, 32, 1, 8, 512, 512], P('tensor', 'shard', None, 'replica')
- right_next: bfloat16 [4, 32, 1, 8, 512, 512], P('tensor', 'shard', None, 'replica')
The draws below stay inside these ranges and needn't reach their ends.
Inputs may be any that keep to these rules, and one draw needn't show every extreme that they name: `block_owner`: worker w stands for shard index w // 8, slot (w // 8) % 1 and replica index w % 8. Among the blocks whose output blocks lie on one index of tensor (a // 4 equal), no worker is named twice, and for one input block b at most 1 of them name workers of one shard index; that bound is reached for every input block. `left_stat`: each slot's matrix is symmetric positive semidefinite. `right_stat`: each slot's matrix is symmetric positive semidefinite.
All inputs are finite; a program needn't handle non-finite values.
Results may differ from the reference program's by a relative error of at most 0.015.
Values may be sent and summed in bfloat16 or wider, within the bound.
A program may use at most 32 MiB of HBM per device.

```python
import math
import jax
import jax.numpy as jnp
from jax import lax

BLOCK = 512
LAYERS = 2
OBT = 4
ITERS = 2
OB = 16
D = 4096
SLOTS = 1
N_TENSOR = 4
N_SHARD = 32
N_REPLICA = 8


def one_group(group_key):
    per_shard = N_REPLICA * SLOTS
    shared = LAYERS * OBT
    inner_count = N_SHARD // 4
    offset = jax.random.randint(jax.random.fold_in(group_key, 1), (), 0, N_SHARD)
    orders = jax.vmap(lambda column: jax.random.permutation(jax.random.fold_in(group_key, 100 + column), shared))(jnp.arange(inner_count))
    position = jnp.arange(inner_count)[:, None] * shared + orders
    owner_shard = (offset + position) % N_SHARD
    shard_rank = position // N_SHARD
    slot_orders = jax.vmap(lambda shard_id: jax.random.permutation(jax.random.fold_in(group_key, 5000 + shard_id), per_shard))(jnp.arange(N_SHARD))
    slot_pick = slot_orders[owner_shard, shard_rank]
    worker = owner_shard * per_shard + slot_pick
    return worker.T.reshape(LAYERS, OBT, inner_count)


def draw_block_owner(key, part):
    groups = jax.vmap(lambda tensor_id: one_group(jax.random.fold_in(key, 7 + tensor_id)))(jnp.arange(N_TENSOR))
    groups = groups.transpose(1, 0, 2, 3).reshape(LAYERS, N_TENSOR * OBT, N_SHARD // 4)
    return groups.astype(jnp.int32)


def stat_field(base_key):
    count = N_TENSOR * N_SHARD * SLOTS * N_REPLICA

    def one_slot(index):
        sub_key = jax.random.fold_in(base_key, index)
        factor = jax.random.normal(sub_key, (BLOCK, BLOCK), jnp.float32) * math.sqrt(8.0)
        return jnp.dot(factor, factor.T, precision=lax.Precision.HIGHEST)
    stats = lax.map(one_slot, jnp.arange(count))
    return stats.reshape(N_TENSOR, N_SHARD, SLOTS, N_REPLICA, BLOCK, BLOCK).astype(jnp.bfloat16)


def draw_left_stat(key, part):
    return stat_field(jax.random.fold_in(key, 11))


def draw_right_stat(key, part):
    return stat_field(jax.random.fold_in(key, 12))


def block_scale(key, dims, pieces, low, top_value):
    loudness = 1.0
    for dim, shards_of in pieces:
        heights = jax.random.uniform(jax.random.fold_in(jax.random.fold_in(key, 6), dim), (shards_of,), jnp.float32, low / len(pieces), top_value / len(pieces))
        loudness = loudness * jnp.repeat(jnp.exp(heights), dims[dim] // shards_of).reshape((-1,) + (1,) * (len(dims) - 1 - dim))
    return loudness


def noise(rng, shape, width, most, split=(), kind=jnp.bfloat16):
    values = width * jax.random.normal(rng, shape, jnp.float32)
    if split:
        values = values * block_scale(rng, shape, split, -0.22, 0.18)
    return jnp.clip(values, -most, most).astype(kind)


def setup_inputs(seed: int = 0) -> dict:
    streams_of = jax.random.split(jax.random.key(seed), 5)
    return {
        "grad_parts": noise(streams_of[0], (N_REPLICA, LAYERS, OB, BLOCK, D), 1.0, 6.0, ((0, 8), (2, 4), (4, 32))),
        "block_owner": draw_block_owner(jax.random.fold_in(streams_of[4], 71), 0),
        "left_stat": draw_left_stat(jax.random.fold_in(streams_of[4], 71), 0),
        "right_stat": draw_right_stat(jax.random.fold_in(streams_of[4], 71), 0),
    }


damping = 0.1
epsilon = 1e-06
decay = 0.9

def matmul(first_op, second_op):
    return jnp.dot(first_op, second_op, preferred_element_type=jnp.float32)

def inverse_root(factor, energy):
    identity = jnp.eye(BLOCK, dtype=jnp.float32)
    shifted = factor + damping * (energy / BLOCK + epsilon) * identity
    scaling = jnp.sqrt(jnp.sum(shifted * shifted))
    coupled = shifted / scaling
    estimate = coupled
    for sweep in range(ITERS):
        stepper = (5.0 * identity - coupled) / 4.0
        stepper_low = stepper.astype(jnp.bfloat16)
        if sweep == 0:
            estimate = stepper
        else:
            estimate = matmul(estimate.astype(jnp.bfloat16), stepper_low)
        if sweep + 1 < ITERS:
            squared = matmul(stepper_low, stepper_low).astype(jnp.bfloat16)
            quartic = matmul(squared, squared).astype(jnp.bfloat16)
            coupled = matmul(quartic, coupled.astype(jnp.bfloat16))
    return estimate.astype(jnp.bfloat16)

def precondition_one(operands):
    block_tile, left_prev, right_prev = operands
    left_gram = decay * left_prev.astype(jnp.float32) + matmul(block_tile, block_tile.T)
    right_gram = decay * right_prev.astype(jnp.float32) + matmul(block_tile.T, block_tile)
    energy = jnp.sum(jnp.square(block_tile.astype(jnp.float32)))
    left_root = inverse_root(left_gram, energy)
    right_root = inverse_root(right_gram, energy)
    half_step = matmul(left_root, block_tile).astype(jnp.bfloat16)
    raw_update = matmul(half_step, right_root)
    mean_grad = energy / (BLOCK * BLOCK)
    mean_raw = jnp.mean(raw_update * raw_update)
    graft_scale = jnp.sqrt((mean_grad + epsilon) / (mean_raw + epsilon))
    result = (raw_update * graft_scale).astype(jnp.bfloat16)
    left_trace = jnp.sum(jnp.diagonal(left_gram))
    stat_rms = jnp.sqrt(left_trace / (BLOCK * BLOCK))
    return (result, stat_rms, left_gram.astype(jnp.bfloat16), right_gram.astype(jnp.bfloat16))

def reference(grad_parts, block_owner, left_stat, right_stat):
    summed = lax.optimization_barrier(jnp.sum(grad_parts.astype(jnp.float32), axis=0)).astype(jnp.bfloat16)
    outer_count = summed.shape[1]
    inner_count = summed.shape[3] // BLOCK
    tiles_all = summed.reshape(LAYERS, outer_count, BLOCK, inner_count, BLOCK)
    tiles_all = tiles_all.transpose(0, 1, 3, 2, 4).reshape(-1, BLOCK, BLOCK)
    workers = N_SHARD * N_REPLICA * SLOTS
    tensor_of = (jnp.arange(outer_count) // OBT).astype(jnp.int32)
    slot_index = (tensor_of[None, :, None] * workers + block_owner.astype(jnp.int32)).reshape(-1).astype(jnp.int32)
    left_flat = left_stat.reshape(N_TENSOR * workers, BLOCK, BLOCK)
    right_flat = right_stat.reshape(N_TENSOR * workers, BLOCK, BLOCK)
    updated, block_norms, left_new, right_new = lax.map(precondition_one, (tiles_all, left_flat[slot_index], right_flat[slot_index]))
    update = updated.reshape(LAYERS, outer_count, inner_count, BLOCK, BLOCK)
    update = update.transpose(0, 1, 3, 2, 4).reshape(LAYERS, outer_count, BLOCK, inner_count * BLOCK)
    diag_prev = jnp.diagonal(left_flat, axis1=1, axis2=2).astype(jnp.float32)
    rms_table = jnp.sqrt(lax.optimization_barrier(jnp.sum(decay * diag_prev, axis=1)) / (BLOCK * BLOCK))
    rms_table = rms_table.at[slot_index].set(block_norms.astype(jnp.float32))
    block_rms = rms_table.reshape(N_TENSOR, N_SHARD, SLOTS, N_REPLICA)
    left_next = (decay * left_flat.astype(jnp.float32)).astype(jnp.bfloat16).at[slot_index].set(left_new)
    right_next = (decay * right_flat.astype(jnp.float32)).astype(jnp.bfloat16).at[slot_index].set(right_new)
    left_next = left_next.reshape(left_stat.shape)
    right_next = right_next.reshape(right_stat.shape)
    return (update, block_rms, left_next, right_next)
```

```python
import jax
import jax.numpy as jnp
from jax import lax
from jax.experimental import pallas as pl
from jax.experimental.pallas import tpu as pltpu
from jax.sharding import PartitionSpec as P

LAYERS = 2
OBT = 4
ITERS = 2


damping = 0.1
epsilon = 1e-06
decay = 0.9


def split_up(shard, dim, length):
    before, after = (shard.shape[:dim], shard.shape[dim + 1 :])
    return jnp.moveaxis(shard.reshape(*before, length, -1, *after), dim, 0)


def summed_on_arrival(shard, axis, dim):
    parts = split_up(shard, dim, lax.axis_size(axis))
    arrived = lax.all_to_all(parts, axis, split_axis=0, concat_axis=0, tiled=True)
    return arrived.astype(jnp.float32).sum(axis=0)


def batched(first_op, second_op, pattern):
    return jnp.einsum(pattern, first_op, second_op, preferred_element_type=jnp.float32)


def inverse_root(factor, energy, extent):
    identity = jnp.eye(extent, dtype=jnp.float32)
    shifted = factor + (damping * (energy / extent + epsilon))[:, None, None] * identity
    scaling = jnp.sqrt(jnp.sum(shifted * shifted, axis=(1, 2), keepdims=True))
    coupled = shifted / scaling
    estimate = coupled
    for sweep in range(ITERS):
        stepper = (5.0 * identity - coupled) / 4.0
        stepper_low = stepper.astype(jnp.bfloat16)
        if sweep == 0:
            estimate = stepper
        else:
            estimate = batched(estimate.astype(jnp.bfloat16), stepper_low, "sij,sjk->sik")
        if sweep + 1 < ITERS:
            squared = batched(stepper_low, stepper_low, "sij,sjk->sik").astype(jnp.bfloat16)
            quartic = batched(squared, squared, "sij,sjk->sik").astype(jnp.bfloat16)
            coupled = batched(quartic, coupled.astype(jnp.bfloat16), "sij,sjk->sik")
    return estimate.astype(jnp.bfloat16)


def precondition(blocks, left_prev, right_prev):
    extent = blocks.shape[-1]
    left_gram = decay * left_prev.astype(jnp.float32) + batched(blocks, blocks, "sij,skj->sik")
    right_gram = decay * right_prev.astype(jnp.float32) + batched(blocks, blocks, "sji,sjk->sik")
    energy = jnp.sum(jnp.square(blocks.astype(jnp.float32)), axis=(1, 2))
    left_root = inverse_root(left_gram, energy, extent)
    right_root = inverse_root(right_gram, energy, extent)
    half_step = batched(left_root, blocks, "sij,sjk->sik").astype(jnp.bfloat16)
    raw_update = batched(half_step, right_root, "sij,sjk->sik")
    mean_grad = energy / (extent * extent)
    mean_raw = jnp.mean(raw_update * raw_update, axis=(1, 2))
    graft_scale = jnp.sqrt((mean_grad + epsilon) / (mean_raw + epsilon))
    result = (raw_update * graft_scale[:, None, None]).astype(jnp.bfloat16)
    left_trace = jnp.sum(jnp.diagonal(left_gram, axis1=1, axis2=2), axis=1)
    stat_rms = jnp.sqrt(left_trace / (extent * extent))
    return (result, stat_rms, left_gram.astype(jnp.bfloat16), right_gram.astype(jnp.bfloat16))


def routing(block_owner, shards, per_shard, capacity, my_shard, ways):
    shared = block_owner.shape[0] * block_owner.shape[1]
    columns = block_owner.shape[2]
    flat_owner = block_owner.reshape(shared, columns)
    dest_shard = flat_owner // per_shard
    order_ids = jnp.arange(shared)
    earlier = order_ids[:, None] < order_ids[None, :]
    same_dest = dest_shard[:, None, :] == dest_shard[None, :, :]
    send_rank = jnp.sum((same_dest & earlier[:, :, None]).astype(jnp.int32), axis=0)
    column_hit = jnp.arange(columns) == my_shard // ways
    my_dest = jnp.sum(jnp.where(column_hit[None, :], dest_shard, 0), axis=1)
    my_rank = jnp.sum(jnp.where(column_hit[None, :], send_rank, 0), axis=1)
    shard_ids = jnp.arange(shards)
    cap_ids = jnp.arange(capacity)
    select_send = (my_dest[None, None, :] == shard_ids[:, None, None]) & (
        my_rank[None, None, :] == cap_ids[None, :, None]
    )
    select_send = select_send.reshape(shards * capacity, shared).astype(jnp.bfloat16)
    slot_ids = my_shard * per_shard + jnp.arange(per_shard)
    slot_match = (flat_owner[None, :, :] == slot_ids[:, None, None]).astype(jnp.float32)
    side_table = (
        shard_ids[None, None, :]
        == ways * jnp.arange(columns)[:, None, None] + jnp.arange(ways)[None, :, None]
    ).astype(jnp.float32)
    rank_table = (send_rank[:, :, None] == cap_ids[None, None, :]).astype(jnp.float32)
    chooser = jnp.einsum("umb,bhs,mbc->uhsc", slot_match, side_table, rank_table)
    chooser = chooser.reshape(per_shard * ways, shards * capacity).astype(jnp.bfloat16)
    return (select_send, chooser)


def general_path(grad_parts, block_owner, left_stat, right_stat):
    replicas = lax.axis_size("replica")
    shards = lax.axis_size("shard")
    my_shard = lax.axis_index("shard")
    extent = grad_parts.shape[3]
    part_cols = grad_parts.shape[4]
    ways = extent // part_cols
    strip_rows = extent // replicas
    shared = LAYERS * OBT
    capacity = (shared + shards - 1) // shards
    slot_count = (shared // ways + replicas - 1) // replicas
    per_shard = slot_count * replicas
    piece_size = strip_rows * part_cols
    grouped = grad_parts.reshape(LAYERS, OBT, replicas, strip_rows, part_cols)
    summed = summed_on_arrival(grouped, "replica", 2)
    pieces = summed.astype(jnp.bfloat16).reshape(shared, piece_size)
    select_send, chooser = routing(block_owner, shards, per_shard, capacity, my_shard, ways)
    outgoing = jnp.dot(select_send, pieces, preferred_element_type=jnp.float32).astype(jnp.bfloat16)
    outgoing = outgoing.reshape(shards, capacity, strip_rows, part_cols)
    arrived = lax.all_to_all(outgoing, "shard", split_axis=0, concat_axis=0, tiled=True)
    gathered = jnp.dot(
        chooser, arrived.reshape(shards * capacity, piece_size), preferred_element_type=jnp.float32
    ).astype(jnp.bfloat16)
    gathered = gathered.reshape(per_shard, ways, strip_rows, part_cols).transpose(0, 2, 1, 3)
    gathered = gathered.reshape(slot_count, replicas, strip_rows, extent)
    blocks = lax.all_to_all(gathered, "replica", split_axis=1, concat_axis=1, tiled=True).reshape(
        slot_count, extent, extent
    )
    left_prev = left_stat.reshape(slot_count, extent, extent)
    right_prev = right_stat.reshape(slot_count, extent, extent)
    updated, block_norms, left_next, right_next = precondition(blocks, left_prev, right_prev)
    spread = lax.all_to_all(
        updated.reshape(slot_count, replicas, strip_rows, extent),
        "replica",
        split_axis=1,
        concat_axis=1,
        tiled=True,
    )
    spread = (
        spread.reshape(per_shard, strip_rows, ways, part_cols)
        .transpose(0, 2, 1, 3)
        .reshape(per_shard * ways, piece_size)
    )
    outgoing_back = jnp.dot(chooser.T, spread, preferred_element_type=jnp.float32).astype(
        jnp.bfloat16
    )
    outgoing_back = outgoing_back.reshape(shards, capacity, strip_rows, part_cols)
    returned = lax.all_to_all(outgoing_back, "shard", split_axis=0, concat_axis=0, tiled=True)
    mine = jnp.dot(
        select_send.T,
        returned.reshape(shards * capacity, piece_size),
        preferred_element_type=jnp.float32,
    ).astype(jnp.bfloat16)
    state_shape = (1, 1, slot_count, 1, extent, extent)
    return (
        mine.reshape(LAYERS, OBT, strip_rows, part_cols),
        block_norms.reshape(1, 1, slot_count, 1),
        left_next.reshape(state_shape),
        right_next.reshape(state_shape),
    )


BLOCK = 512
SHARDS = 32
REPL = 8
TENSORS = 4
WAYS = 4
GROUPS = 8
SHARED = 8
CAP = 2
STRIP = 64
COLS = 128
SLICE = 8
RB = 128
MESH = pl.DeviceIdType.MESH
VMEM = pltpu.VMEM
DMA = pltpu.SemaphoreType.DMA
FAR = [16] + [d for k in range(15, 0, -1) for d in (k, SHARDS - k)]
FAR_GROUPS = [4, 3, 5, 2, 6, 1, 7]


def wrap(value, extent):
    return lax.rem(value, extent)


def diagonal(block):
    rows = lax.broadcasted_iota(jnp.int32, (RB, BLOCK), 0) + block * RB
    return rows == lax.broadcasted_iota(jnp.int32, (RB, BLOCK), 1)


def total(value):
    return jnp.sum(value, axis=(0, 1), keepdims=True)


def step_kernel(
    tab,
    flag_ref,
    grads,
    left_stat,
    right_stat,
    update,
    rms,
    left_next,
    right_next,
    flags_out,
    flags,
    partial,
    summed,
    spread,
    picked,
    landed,
    packed,
    strips,
    block,
    block_t,
    stat,
    gram,
    nxt,
    coup,
    low1,
    low2,
    quart,
    raw,
    tiles,
    back,
    vpack,
    home,
    hpack,
    final,
    local_sem,
    flag_send,
    flag_recv,
    rs_send,
    rs_recv,
    s1_send,
    s1_recv,
    s2_send,
    s2_recv,
    s4_send,
    s4_recv,
    b4_send,
    b4_recv,
    b2_send,
    b2_recv,
    b1_send,
    b1_recv,
):
    t = lax.axis_index("tensor")
    z = lax.axis_index("shard")
    r = lax.axis_index("replica")
    my_group = z // WAYS
    my_lane = wrap(z, WAYS)

    stat_in = [
        pltpu.make_async_copy(left_stat, stat.at[0], local_sem.at[0]),
        pltpu.make_async_copy(right_stat, stat.at[1], local_sem.at[1]),
    ]
    for copy in stat_in:
        copy.start()

    barrier = pltpu.get_barrier_semaphore()
    for d in FAR:
        pl.semaphore_signal(
            barrier, inc=1, device_id={"shard": wrap(z + d, SHARDS)}, device_id_type=MESH
        )
    for d in range(1, REPL):
        pl.semaphore_signal(
            barrier, inc=1, device_id={"replica": wrap(r + d, REPL)}, device_id_type=MESH
        )
    for d in range(1, TENSORS):
        pl.semaphore_signal(
            barrier, inc=1, device_id={"tensor": wrap(t + d, TENSORS)}, device_id_type=MESH
        )
    pl.semaphore_wait(barrier, SHARDS + REPL + TENSORS - 3)

    def remote(src, dst, send, recv, axis, peer):
        return pltpu.make_async_remote_copy(
            src_ref=src,
            dst_ref=dst,
            send_sem=send,
            recv_sem=recv,
            device_id={axis: peer},
            device_id_type=MESH,
        )

    sent = []

    rs_copies = []
    for d in range(1, REPL):
        peer = wrap(r + d, REPL)
        rs_copies.append(
            remote(
                grads.at[:, pl.ds(pl.multiple_of(peer * STRIP, STRIP), STRIP), :],
                partial.at[d],
                rs_send.at[d],
                rs_recv.at[d],
                "replica",
                peer,
            )
        )
    for copy in rs_copies:
        copy.start()
    own = pltpu.make_async_copy(
        grads.at[:, pl.ds(pl.multiple_of(r * STRIP, STRIP), STRIP), :],
        partial.at[0],
        local_sem.at[2],
    )
    own.start()
    flag_copies = []
    for d in range(1, TENSORS):
        flag_copies.append(
            remote(
                flag_ref, flags.at[d], flag_send.at[d], flag_recv.at[d],
                "tensor", wrap(t + d, TENSORS),
            )
        )
    for copy in flag_copies:
        copy.start()
    sent += rs_copies + flag_copies
    own.wait()
    for copy in rs_copies:
        copy.wait_recv()
    for i in range(SHARED):
        acc = partial[0, i].astype(jnp.float32)
        for d in range(1, REPL):
            acc = acc + partial[d, i].astype(jnp.float32)
        summed[:, i] = acc.reshape(GROUPS, SLICE, COLS).astype(jnp.bfloat16)

    s1_copies = []
    for d in FAR_GROUPS:
        m = wrap(my_group + d, GROUPS)
        s1_copies.append(
            remote(
                summed.at[m], spread.at[my_group], s1_send.at[d], s1_recv.at[d],
                "shard", m * WAYS + my_lane,
            )
        )
    for copy in s1_copies:
        copy.start()
    sent += s1_copies
    own = pltpu.make_async_copy(summed.at[my_group], spread.at[my_group], local_sem.at[2])
    own.start()
    own.wait()
    for copy in s1_copies:
        copy.wait_recv()

    for p in range(SHARDS * CAP):
        n = tab[0, p]
        picked[p // CAP, p % CAP] = spread[n // SHARED, wrap(n, SHARED)]
    s2_copies = []
    for d in FAR:
        peer = wrap(z + d, SHARDS)
        s2_copies.append(
            remote(
                picked.at[peer], landed.at[:, z], s2_send.at[d], s2_recv.at[d], "shard", peer
            )
        )
    for copy in s2_copies:
        copy.start()
    sent += s2_copies
    own = pltpu.make_async_copy(picked.at[z], landed.at[:, z], local_sem.at[2])
    own.start()
    own.wait()
    for copy in s2_copies:
        copy.wait_recv()

    for w in range(REPL):
        packed[w] = landed[tab[2, w]]
    s4_copies = []
    for d in range(1, REPL):
        peer = wrap(r + d, REPL)
        s4_copies.append(
            remote(
                packed.at[peer], strips.at[r], s4_send.at[d], s4_recv.at[d], "replica", peer
            )
        )
    for copy in s4_copies:
        copy.start()
    sent += s4_copies
    own = pltpu.make_async_copy(packed.at[r], strips.at[r], local_sem.at[2])
    own.start()
    own.wait()
    for copy in s4_copies:
        copy.wait_recv()

    holds = tab[2, 10] > 0
    square_sum = jnp.zeros((STRIP, COLS), jnp.float32)
    for q in range(REPL):
        strip = strips[q].astype(jnp.float32).reshape(GROUPS, WAYS, SLICE, COLS)
        for j in range(WAYS):
            piece = strip[:, j].reshape(STRIP, COLS)
            piece = jnp.where(holds, piece, 0.0)
            square_sum = square_sum + piece * piece
            block[pl.ds(q * STRIP, STRIP), pl.ds(j * COLS, COLS)] = piece.astype(jnp.bfloat16)
    energy = total(square_sum)
    block_t[...] = block[...].T
    for copy in stat_in:
        copy.wait()

    shift = damping * (energy / BLOCK + epsilon)
    scales = []
    for f in range(2):
        side = block if f == 0 else block_t
        other = block_t if f == 0 else block
        squares = jnp.zeros((1, 1), jnp.float32)
        trace = jnp.zeros((1, 1), jnp.float32)
        for i in range(BLOCK // RB):
            rows = pl.ds(i * RB, RB)
            value = decay * stat[f, rows, :].astype(jnp.float32) + jnp.dot(
                side[rows, :], other[...], preferred_element_type=jnp.float32
            )
            gram[f, rows, :] = value
            nxt[f, rows, :] = value.astype(jnp.bfloat16)
            squares = squares + total(value * value)
            trace = trace + total(jnp.where(diagonal(i), value, 0.0))
        if f == 0:
            rms[...] = jnp.broadcast_to(jnp.sqrt(trace / (BLOCK * BLOCK)), rms.shape)
        norm = jnp.sqrt(squares + 2.0 * shift * trace + BLOCK * (shift * shift))
        scales.append(1.0 / norm)
    next_out = [
        pltpu.make_async_copy(nxt.at[0], left_next, local_sem.at[0]),
        pltpu.make_async_copy(nxt.at[1], right_next, local_sem.at[1]),
    ]
    for copy in next_out:
        copy.start()

    for i in range(BLOCK // RB):
        rows = pl.ds(i * RB, RB)
        eye = diagonal(i)
        for f in range(2):
            coupled = (gram[f, rows, :] + jnp.where(eye, shift, 0.0)) * scales[f]
            coup[f, rows, :] = coupled.astype(jnp.bfloat16)
            stepper = (jnp.where(eye, 5.0, 0.0) - coupled) * 0.25
            low1[f, rows, :] = stepper.astype(jnp.bfloat16)

    def product(left, right, i):
        return jnp.dot(
            left[pl.ds(i * RB, RB), :], right[...], preferred_element_type=jnp.float32
        )

    for i in range(BLOCK // RB):
        for f in range(2):
            low2[f, pl.ds(i * RB, RB), :] = product(low1.at[f], low1.at[f], i).astype(
                jnp.bfloat16
            )
    for i in range(BLOCK // RB):
        for f in range(2):
            quart[f, pl.ds(i * RB, RB), :] = product(low2.at[f], low2.at[f], i).astype(
                jnp.bfloat16
            )
    for i in range(BLOCK // RB):
        eye = diagonal(i)
        for f in range(2):
            coupled = product(quart.at[f], coup.at[f], i)
            stepper = (jnp.where(eye, 5.0, 0.0) - coupled) * 0.25
            low2[f, pl.ds(i * RB, RB), :] = stepper.astype(jnp.bfloat16)
    for i in range(BLOCK // RB):
        for f in range(2):
            quart[f, pl.ds(i * RB, RB), :] = product(low1.at[f], low2.at[f], i).astype(
                jnp.bfloat16
            )
    for i in range(BLOCK // RB):
        coup[0, pl.ds(i * RB, RB), :] = product(quart.at[0], block, i).astype(jnp.bfloat16)
    raw_sum = jnp.zeros((1, 1), jnp.float32)
    for i in range(BLOCK // RB):
        value = product(coup.at[0], quart.at[1], i)
        raw[pl.ds(i * RB, RB), :] = value
        raw_sum = raw_sum + total(value * value)
    size = float(BLOCK * BLOCK)
    graft = jnp.sqrt((energy / size + epsilon) / (raw_sum / size + epsilon))
    for q in range(REPL):
        for j in range(WAYS):
            piece = raw[pl.ds(q * STRIP, STRIP), pl.ds(j * COLS, COLS)] * graft
            tiles[q, :, j] = piece.reshape(GROUPS, SLICE, COLS).astype(jnp.bfloat16)

    b4_copies = []
    for d in range(1, REPL):
        peer = wrap(r + d, REPL)
        b4_copies.append(
            remote(tiles.at[peer], back.at[r], b4_send.at[d], b4_recv.at[d], "replica", peer)
        )
    for copy in b4_copies:
        copy.start()
    sent += b4_copies
    own = pltpu.make_async_copy(tiles.at[r], back.at[r], local_sem.at[2])
    own.start()
    own.wait()
    for copy in b4_copies:
        copy.wait_recv()

    for k in range(CAP):
        vpack[:, :, k] = back[tab[2, 8 + k]]
    b2_copies = []
    for d in FAR:
        peer = wrap(z + d, SHARDS)
        b2_copies.append(
            remote(
                vpack.at[peer // WAYS, wrap(peer, WAYS)], home.at[z], b2_send.at[d],
                b2_recv.at[d], "shard", peer,
            )
        )
    for copy in b2_copies:
        copy.start()
    sent += b2_copies
    own = pltpu.make_async_copy(vpack.at[my_group, my_lane], home.at[z], local_sem.at[2])
    own.start()
    own.wait()
    for copy in b2_copies:
        copy.wait_recv()

    for n in range(SHARED * GROUPS):
        pos = tab[1, n]
        hpack[n // SHARED, n % SHARED] = home[pos // CAP, wrap(pos, CAP)]
    b1_copies = []
    for d in FAR_GROUPS:
        m = wrap(my_group + d, GROUPS)
        b1_copies.append(
            remote(
                hpack.at[m], final.at[my_group], b1_send.at[d], b1_recv.at[d],
                "shard", m * WAYS + my_lane,
            )
        )
    for copy in b1_copies:
        copy.start()
    sent += b1_copies
    own = pltpu.make_async_copy(hpack.at[my_group], final.at[my_group], local_sem.at[2])
    own.start()
    own.wait()
    for copy in b1_copies:
        copy.wait_recv()
    for i in range(SHARED):
        piece = final[:, i].astype(jnp.float32).reshape(STRIP, COLS)
        update[i] = piece.astype(jnp.bfloat16)

    flags_out[0] = flag_ref[...]
    for copy in flag_copies:
        copy.wait_recv()
    for d in range(1, TENSORS):
        flags_out[d] = flags[d]
    for copy in next_out:
        copy.wait()
    for copy in sent:
        copy.wait_send()


def tables(block_owner):
    owner = block_owner.reshape(SHARED, GROUPS).T.reshape(-1)
    count = SHARED * GROUPS
    ids = jnp.arange(count)
    dest = owner // REPL
    same = dest[:, None] == dest[None, :]
    rank = jnp.sum((same & (ids[:, None] < ids[None, :])).astype(jnp.int32), axis=0)
    balanced = jnp.all(rank < CAP)
    rank = jnp.minimum(rank, CAP - 1)
    place = dest * CAP + rank
    inverse = jnp.sum(jnp.where(place[None, :] == ids[:, None], ids[None, :], 0), axis=1)
    inverse = jnp.minimum(inverse, count - 1)
    shard = lax.axis_index("shard")
    me = shard * REPL + lax.axis_index("replica")
    q = ids[:, None]
    chosen = jnp.where(
        q < REPL,
        jnp.where(owner[None, :] == shard * REPL + q, rank[None, :], 0),
        jnp.where(
            q < REPL + CAP,
            jnp.where(place[None, :] == shard * CAP + q - REPL, (owner % REPL)[None, :], 0),
            (owner == me).astype(jnp.int32)[None, :],
        ),
    )
    misc = jnp.minimum(jnp.sum(chosen, axis=1), REPL - 1)
    return jnp.stack([inverse, place, misc]), balanced


def balanced_path(table, balanced, grads, left_stat, right_stat):
    bf16, f32 = jnp.bfloat16, jnp.float32
    any_space = pl.BlockSpec(memory_space=pl.ANY)
    vmem = pl.BlockSpec(memory_space=VMEM)
    flag = jnp.full((8, 128), balanced.astype(jnp.int32))
    square = (BLOCK, BLOCK)
    return pl.pallas_call(
        step_kernel,
        out_shape=(
            jax.ShapeDtypeStruct((SHARED, STRIP, COLS), bf16),
            jax.ShapeDtypeStruct((8, 128), f32),
            jax.ShapeDtypeStruct(square, bf16),
            jax.ShapeDtypeStruct(square, bf16),
            jax.ShapeDtypeStruct((TENSORS, 8, 128), jnp.int32),
        ),
        in_specs=[
            pl.BlockSpec(memory_space=pltpu.SMEM),
            vmem,
            any_space,
            any_space,
            any_space,
        ],
        out_specs=(vmem, vmem, any_space, any_space, vmem),
        scratch_shapes=[
            VMEM((TENSORS, 8, 128), jnp.int32),
            VMEM((REPL, SHARED, STRIP, COLS), bf16),
            VMEM((GROUPS, SHARED, SLICE, COLS), bf16),
            VMEM((GROUPS, SHARED, SLICE, COLS), bf16),
            VMEM((SHARDS, CAP, SLICE, COLS), bf16),
            VMEM((CAP, SHARDS, SLICE, COLS), bf16),
            VMEM((REPL, SHARDS, SLICE, COLS), bf16),
            VMEM((REPL, SHARDS, SLICE, COLS), bf16),
            VMEM(square, bf16),
            VMEM(square, bf16),
            VMEM((2,) + square, bf16),
            VMEM((2,) + square, f32),
            VMEM((2,) + square, bf16),
            VMEM((2,) + square, bf16),
            VMEM((2,) + square, bf16),
            VMEM((2,) + square, bf16),
            VMEM((2,) + square, bf16),
            VMEM(square, f32),
            VMEM((REPL, GROUPS, WAYS, SLICE, COLS), bf16),
            VMEM((REPL, GROUPS, WAYS, SLICE, COLS), bf16),
            VMEM((GROUPS, WAYS, CAP, SLICE, COLS), bf16),
            VMEM((SHARDS, CAP, SLICE, COLS), bf16),
            VMEM((GROUPS, SHARED, SLICE, COLS), bf16),
            VMEM((GROUPS, SHARED, SLICE, COLS), bf16),
            DMA((3,)),
            DMA((TENSORS,)),
            DMA((TENSORS,)),
            DMA((REPL,)),
            DMA((REPL,)),
            DMA((GROUPS,)),
            DMA((GROUPS,)),
            DMA((SHARDS,)),
            DMA((SHARDS,)),
            DMA((REPL,)),
            DMA((REPL,)),
            DMA((REPL,)),
            DMA((REPL,)),
            DMA((SHARDS,)),
            DMA((SHARDS,)),
            DMA((GROUPS,)),
            DMA((GROUPS,)),
        ],
        compiler_params=pltpu.CompilerParams(
            collective_id=0, has_side_effects=True, vmem_limit_bytes=40 << 20
        ),
    )(table, flag, grads, left_stat, right_stat)


def per_device(grad_parts, block_owner, left_stat, right_stat):
    table, balanced = tables(block_owner)
    square = (BLOCK, BLOCK)
    update, rms, left_next, right_next, flags = balanced_path(
        table,
        balanced,
        grad_parts.reshape(SHARED, BLOCK, COLS),
        left_stat.reshape(square),
        right_stat.reshape(square),
    )
    state_shape = (1, 1, 1, 1, BLOCK, BLOCK)
    found = (
        update.reshape(LAYERS, OBT, STRIP, COLS),
        rms[:1, :1].reshape(1, 1, 1, 1),
        left_next.reshape(state_shape),
        right_next.reshape(state_shape),
    )
    return lax.cond(
        jnp.min(flags[:, 0, 0]) > 0,
        lambda *_: found,
        general_path,
        grad_parts,
        block_owner,
        left_stat,
        right_stat,
    )


def solution(mesh):
    return jax.shard_map(
        per_device,
        mesh=mesh,
        in_specs=(
            P("replica", None, "tensor", None, "shard"),
            P(None, "tensor", None),
            P("tensor", "shard", None, "replica", None, None),
            P("tensor", "shard", None, "replica", None, None),
        ),
        out_specs=(
            P(None, "tensor", "replica", "shard"),
            P("tensor", "shard", None, "replica"),
            P("tensor", "shard", None, "replica", None, None),
            P("tensor", "shard", None, "replica", None, None),
        ),
        check_vma=False,
    )
```

```python
import jax
import jax.numpy as jnp
from jax import lax
from jax.experimental import pallas as pl
from jax.experimental.pallas import tpu as pltpu
from jax.sharding import PartitionSpec as P

LAYERS = 2
OBT = 4
ITERS = 2


damping = 0.1
epsilon = 1e-06
decay = 0.9


def split_up(shard, dim, length):
    before, after = (shard.shape[:dim], shard.shape[dim + 1 :])
    return jnp.moveaxis(shard.reshape(*before, length, -1, *after), dim, 0)


def summed_on_arrival(shard, axis, dim):
    parts = split_up(shard, dim, lax.axis_size(axis))
    arrived = lax.all_to_all(parts, axis, split_axis=0, concat_axis=0, tiled=True)
    return arrived.astype(jnp.float32).sum(axis=0)


def batched(first_op, second_op, pattern):
    return jnp.einsum(pattern, first_op, second_op, preferred_element_type=jnp.float32)


def inverse_root(factor, energy, extent):
    identity = jnp.eye(extent, dtype=jnp.float32)
    shifted = factor + (damping * (energy / extent + epsilon))[:, None, None] * identity
    scaling = jnp.sqrt(jnp.sum(shifted * shifted, axis=(1, 2), keepdims=True))
    coupled = shifted / scaling
    estimate = coupled
    for sweep in range(ITERS):
        stepper = (5.0 * identity - coupled) / 4.0
        stepper_low = stepper.astype(jnp.bfloat16)
        if sweep == 0:
            estimate = stepper
        else:
            estimate = batched(estimate.astype(jnp.bfloat16), stepper_low, "sij,sjk->sik")
        if sweep + 1 < ITERS:
            squared = batched(stepper_low, stepper_low, "sij,sjk->sik").astype(jnp.bfloat16)
            quartic = batched(squared, squared, "sij,sjk->sik").astype(jnp.bfloat16)
            coupled = batched(quartic, coupled.astype(jnp.bfloat16), "sij,sjk->sik")
    return estimate.astype(jnp.bfloat16)


def precondition(blocks, left_prev, right_prev):
    extent = blocks.shape[-1]
    left_gram = decay * left_prev.astype(jnp.float32) + batched(blocks, blocks, "sij,skj->sik")
    right_gram = decay * right_prev.astype(jnp.float32) + batched(blocks, blocks, "sji,sjk->sik")
    energy = jnp.sum(jnp.square(blocks.astype(jnp.float32)), axis=(1, 2))
    left_root = inverse_root(left_gram, energy, extent)
    right_root = inverse_root(right_gram, energy, extent)
    half_step = batched(left_root, blocks, "sij,sjk->sik").astype(jnp.bfloat16)
    raw_update = batched(half_step, right_root, "sij,sjk->sik")
    mean_grad = energy / (extent * extent)
    mean_raw = jnp.mean(raw_update * raw_update, axis=(1, 2))
    graft_scale = jnp.sqrt((mean_grad + epsilon) / (mean_raw + epsilon))
    result = (raw_update * graft_scale[:, None, None]).astype(jnp.bfloat16)
    left_trace = jnp.sum(jnp.diagonal(left_gram, axis1=1, axis2=2), axis=1)
    stat_rms = jnp.sqrt(left_trace / (extent * extent))
    return (result, stat_rms, left_gram.astype(jnp.bfloat16), right_gram.astype(jnp.bfloat16))


def routing(block_owner, shards, per_shard, capacity, my_shard, ways):
    shared = block_owner.shape[0] * block_owner.shape[1]
    columns = block_owner.shape[2]
    flat_owner = block_owner.reshape(shared, columns)
    dest_shard = flat_owner // per_shard
    order_ids = jnp.arange(shared)
    earlier = order_ids[:, None] < order_ids[None, :]
    same_dest = dest_shard[:, None, :] == dest_shard[None, :, :]
    send_rank = jnp.sum((same_dest & earlier[:, :, None]).astype(jnp.int32), axis=0)
    column_hit = jnp.arange(columns) == my_shard // ways
    my_dest = jnp.sum(jnp.where(column_hit[None, :], dest_shard, 0), axis=1)
    my_rank = jnp.sum(jnp.where(column_hit[None, :], send_rank, 0), axis=1)
    shard_ids = jnp.arange(shards)
    cap_ids = jnp.arange(capacity)
    select_send = (my_dest[None, None, :] == shard_ids[:, None, None]) & (
        my_rank[None, None, :] == cap_ids[None, :, None]
    )
    select_send = select_send.reshape(shards * capacity, shared).astype(jnp.bfloat16)
    slot_ids = my_shard * per_shard + jnp.arange(per_shard)
    slot_match = (flat_owner[None, :, :] == slot_ids[:, None, None]).astype(jnp.float32)
    side_table = (
        shard_ids[None, None, :]
        == ways * jnp.arange(columns)[:, None, None] + jnp.arange(ways)[None, :, None]
    ).astype(jnp.float32)
    rank_table = (send_rank[:, :, None] == cap_ids[None, None, :]).astype(jnp.float32)
    chooser = jnp.einsum("umb,bhs,mbc->uhsc", slot_match, side_table, rank_table)
    chooser = chooser.reshape(per_shard * ways, shards * capacity).astype(jnp.bfloat16)
    return (select_send, chooser)


def general_path(grad_parts, block_owner, left_stat, right_stat):
    replicas = lax.axis_size("replica")
    shards = lax.axis_size("shard")
    my_shard = lax.axis_index("shard")
    extent = grad_parts.shape[3]
    part_cols = grad_parts.shape[4]
    ways = extent // part_cols
    strip_rows = extent // replicas
    shared = LAYERS * OBT
    capacity = (shared + shards - 1) // shards
    slot_count = (shared // ways + replicas - 1) // replicas
    per_shard = slot_count * replicas
    piece_size = strip_rows * part_cols
    grouped = grad_parts.reshape(LAYERS, OBT, replicas, strip_rows, part_cols)
    summed = summed_on_arrival(grouped, "replica", 2)
    pieces = summed.astype(jnp.bfloat16).reshape(shared, piece_size)
    select_send, chooser = routing(block_owner, shards, per_shard, capacity, my_shard, ways)
    outgoing = jnp.dot(select_send, pieces, preferred_element_type=jnp.float32).astype(jnp.bfloat16)
    outgoing = outgoing.reshape(shards, capacity, strip_rows, part_cols)
    arrived = lax.all_to_all(outgoing, "shard", split_axis=0, concat_axis=0, tiled=True)
    gathered = jnp.dot(
        chooser, arrived.reshape(shards * capacity, piece_size), preferred_element_type=jnp.float32
    ).astype(jnp.bfloat16)
    gathered = gathered.reshape(per_shard, ways, strip_rows, part_cols).transpose(0, 2, 1, 3)
    gathered = gathered.reshape(slot_count, replicas, strip_rows, extent)
    blocks = lax.all_to_all(gathered, "replica", split_axis=1, concat_axis=1, tiled=True).reshape(
        slot_count, extent, extent
    )
    left_prev = left_stat.reshape(slot_count, extent, extent)
    right_prev = right_stat.reshape(slot_count, extent, extent)
    updated, block_norms, left_next, right_next = precondition(blocks, left_prev, right_prev)
    spread = lax.all_to_all(
        updated.reshape(slot_count, replicas, strip_rows, extent),
        "replica",
        split_axis=1,
        concat_axis=1,
        tiled=True,
    )
    spread = (
        spread.reshape(per_shard, strip_rows, ways, part_cols)
        .transpose(0, 2, 1, 3)
        .reshape(per_shard * ways, piece_size)
    )
    outgoing_back = jnp.dot(chooser.T, spread, preferred_element_type=jnp.float32).astype(
        jnp.bfloat16
    )
    outgoing_back = outgoing_back.reshape(shards, capacity, strip_rows, part_cols)
    returned = lax.all_to_all(outgoing_back, "shard", split_axis=0, concat_axis=0, tiled=True)
    mine = jnp.dot(
        select_send.T,
        returned.reshape(shards * capacity, piece_size),
        preferred_element_type=jnp.float32,
    ).astype(jnp.bfloat16)
    state_shape = (1, 1, slot_count, 1, extent, extent)
    return (
        mine.reshape(LAYERS, OBT, strip_rows, part_cols),
        block_norms.reshape(1, 1, slot_count, 1),
        left_next.reshape(state_shape),
        right_next.reshape(state_shape),
    )


BLOCK = 512
SHARDS = 32
REPL = 8
TENSORS = 4
WAYS = 4
GROUPS = 8
SHARED = 8
CAP = 2
STRIP = 64
COLS = 128
SLICE = 8
RB = 128
MESH = pl.DeviceIdType.MESH
VMEM = pltpu.VMEM
DMA = pltpu.SemaphoreType.DMA
FAR = [16] + [d for k in range(15, 0, -1) for d in (k, SHARDS - k)]
FAR_GROUPS = [4, 3, 5, 2, 6, 1, 7]
SCRATCH = dict(
    tab_v=((8, 128), jnp.int32),
    flag=((8, 128), jnp.int32),
    flags=((TENSORS, 8, 128), jnp.int32),
    stat=((2, BLOCK, BLOCK), jnp.bfloat16),
    tv=((REPL, SHARDS + 1, SLICE, COLS), jnp.bfloat16),
    e1=((REPL, SHARDS + 1, SLICE, COLS), jnp.bfloat16),
    e2=((SHARDS, CAP, SLICE, COLS), jnp.bfloat16),
    dg=((SLICE, COLS), jnp.bfloat16),
    mid=((SHARDS, CAP, SLICE, COLS), jnp.bfloat16),
    dgs=((SHARDS, SLICE, COLS), jnp.bfloat16),
    e3=((SHARDS, CAP, SLICE, COLS), jnp.bfloat16),
    e4=((CAP, SHARDS + 1, SLICE, COLS), jnp.bfloat16),
    tin=((REPL, SHARDS + 1, SLICE, COLS), jnp.bfloat16),
    partial=((REPL, SHARED, STRIP, COLS), jnp.bfloat16),
    summed=((GROUPS, SHARED, SLICE, COLS), jnp.bfloat16),
    spread=((GROUPS, SHARED, SLICE, COLS), jnp.bfloat16),
    picked=((SHARDS, CAP, SLICE, COLS), jnp.bfloat16),
    landed=((CAP, SHARDS, SLICE, COLS), jnp.bfloat16),
    packed=((REPL, SHARDS, SLICE, COLS), jnp.bfloat16),
    strips=((REPL, SHARDS, SLICE, COLS), jnp.bfloat16),
    gin=((REPL, WAYS, GROUPS, SLICE, COLS), jnp.bfloat16),
    block=((BLOCK, BLOCK), jnp.bfloat16),
    block_t=((BLOCK, BLOCK), jnp.bfloat16),
    tri=((BLOCK, BLOCK), jnp.bfloat16),
    tri_t=((BLOCK, BLOCK), jnp.bfloat16),
    gram=((2, BLOCK, BLOCK), jnp.float32),
    coup=((2, BLOCK, BLOCK), jnp.bfloat16),
    low1=((2, BLOCK, BLOCK), jnp.bfloat16),
    low2=((2, BLOCK, BLOCK), jnp.bfloat16),
    quart=((2, BLOCK, BLOCK), jnp.bfloat16),
    raw=((BLOCK, BLOCK), jnp.float32),
    tiles=((REPL, WAYS, GROUPS, SLICE, COLS), jnp.bfloat16),
    final=((SHARED, GROUPS, SLICE, COLS), jnp.bfloat16),
)
SEMS = dict(
    local=16,
    fl_s=TENSORS,
    fl_r=TENSORS,
    e1_s=REPL,
    e1_r=REPL,
    e2_s=SHARDS,
    e2_r=SHARDS,
    dg_s=WAYS,
    dg_r=SHARDS,
    e3_s=SHARDS,
    e3_r=SHARDS,
    e4_s=CAP,
    e4_r=REPL,
    rs_s=REPL,
    rs_r=REPL,
    s1_s=GROUPS,
    s1_r=GROUPS,
    s2_s=SHARDS,
    s2_r=SHARDS,
    s4_s=REPL,
    s4_r=REPL,
    gg_s=SHARED,
    gg_r=WAYS * REPL,
    us_s=WAYS * REPL,
    us_r=SHARED,
)


def wrap(value, extent):
    return lax.rem(value, extent)


def total(value):
    return jnp.sum(value, axis=(0, 1), keepdims=True)


def index_grids(i):
    rows = lax.broadcasted_iota(jnp.int32, (RB, BLOCK), 0) + i * RB
    return rows, lax.broadcasted_iota(jnp.int32, (RB, BLOCK), 1)


def home_replica(i):
    core = i // WAYS
    return 2 * ((i % WAYS + 2 * core) % 4) + core


def step_kernel(owner, grads, left_stat, right_stat, update, rms, left_next, right_next, ok, *rest):
    names = list(SCRATCH)
    m = dict(zip(names, rest[: len(names)]))
    rest = rest[len(names) :]
    sem = dict(zip(SEMS, rest[: len(SEMS)]))
    tab, from_left, from_right = rest[len(SEMS) :]
    stat, block, block_t, gram = m["stat"], m["block"], m["block_t"], m["gram"]
    local = sem["local"]

    t = lax.axis_index("tensor")
    z = lax.axis_index("shard")
    r = lax.axis_index("replica")
    group = z // WAYS
    lane = wrap(z, WAYS)
    core = wrap(r, 2)
    computes = r // 2 == wrap(lane + 2 * core, 4)
    my_block = lane + WAYS * core
    up = wrap(z + 1, SHARDS)
    down = wrap(z + SHARDS - 1, SHARDS)

    stat_in = [
        pltpu.make_async_copy(left_stat, stat.at[0], local.at[0]),
        pltpu.make_async_copy(right_stat, stat.at[1], local.at[1]),
    ]
    for copy in stat_in:
        copy.start()

    def remote(src, dst, send, recv, where):
        return pltpu.make_async_remote_copy(
            src_ref=src,
            dst_ref=dst,
            send_sem=send,
            recv_sem=recv,
            device_id=where,
            device_id_type=MESH,
        )

    def signal(semaphore, where):
        pl.semaphore_signal(semaphore, inc=1, device_id=where, device_id_type=MESH)

    barrier = pltpu.get_barrier_semaphore()
    signal(barrier, {"shard": up})
    signal(barrier, {"shard": down})
    for d in range(1, REPL):
        signal(barrier, {"replica": wrap(r + d, REPL)})
    for d in range(1, TENSORS):
        signal(barrier, {"tensor": wrap(t + d, TENSORS)})

    lanes = lax.broadcasted_iota(jnp.int32, (1, 128), 1)
    rows8 = lax.broadcasted_iota(jnp.int32, (SHARED, 128), 0)
    across = jnp.full((1, 128), -8, jnp.int32)
    columns = []
    for b in range(GROUPS):
        column = jnp.zeros((SHARED, 128), jnp.int32)
        for i in range(SHARED):
            value = owner[i // OBT, i % OBT, b]
            across = jnp.where(lanes == b * SHARED + i, value, across)
            column = jnp.where(rows8 == i, value, column)
        columns.append(column)
    down_w = jnp.concatenate(columns, axis=0)
    count = GROUPS * SHARED
    n_down = lax.broadcasted_iota(jnp.int32, (count, 128), 0)
    n_across = lax.broadcasted_iota(jnp.int32, (count, 128), 1)
    dest_down = down_w >> 3
    same = dest_down == (across >> 3)
    rank_across = jnp.sum(
        jnp.where(same & (n_down < n_across), 1, 0), axis=0, keepdims=True
    )
    rank_down = jnp.sum(jnp.where(same & (n_across < n_down), 1, 0), axis=1, keepdims=True)
    most = jnp.max(rank_down, axis=0, keepdims=True)
    m["flag"][...] = jnp.broadcast_to(jnp.where(most < CAP, 1, 0), (8, 128))
    rank_across = jnp.minimum(rank_across, CAP - 1)
    rank_down = jnp.minimum(rank_down, CAP - 1)
    place_down = dest_down * CAP + rank_down
    inverse = jnp.sum(jnp.where(place_down == n_across, n_down, 0), axis=0, keepdims=True)
    pick = jnp.where(
        n_across < REPL,
        jnp.where(down_w == z * REPL + n_across, rank_down, 0),
        jnp.where(
            n_across < REPL + CAP,
            jnp.where(place_down == z * CAP + n_across - REPL, down_w & 7, 0),
            jnp.where(
                n_across == 10,
                jnp.where(down_w == z * REPL + r, 1, 0),
                jnp.where((dest_down == z) & ((n_down >> 3) == r), down_w & 7, 0),
            ),
        ),
    )
    pick = jnp.sum(pick, axis=0, keepdims=True)
    m["tab_v"][0:1, :] = jnp.minimum(inverse, count - 1)
    m["tab_v"][1:2, :] = jnp.clip((across >> 3) * CAP + rank_across, 0, count - 1)
    m["tab_v"][2:3, :] = jnp.minimum(pick, jnp.where(lanes < REPL, CAP - 1, REPL - 1))
    m["tab_v"][3:8, :] = jnp.zeros((5, 128), jnp.int32)
    tab_in = pltpu.make_async_copy(m["tab_v"], tab, local.at[2])
    tab_in.start()

    for copy in stat_in:
        copy.wait()
    rows8 = lax.broadcasted_iota(jnp.int32, (SLICE, COLS), 0)
    eye = lax.broadcasted_iota(jnp.int32, (COLS, COLS), 0) == lax.broadcasted_iota(
        jnp.int32, (COLS, COLS), 1
    )
    edge = jnp.zeros((SLICE, COLS), jnp.float32)
    for q in range(WAYS):
        span = pl.ds(q * COLS, COLS)
        value = jnp.where(eye, stat[1, span, span].astype(jnp.float32), 0.0)
        edge = jnp.where(rows8 == q, jnp.sum(value, axis=0, keepdims=True), edge)
    for i in range(BLOCK // RB):
        span = pl.ds(i * RB, RB)
        at_row, at_col = index_grids(i)
        value = jnp.where(
            at_row <= at_col,
            stat[0, span, :].astype(jnp.float32),
            stat[1, span, :].astype(jnp.float32),
        )
        for h in range(RB // STRIP):
            p = i * (RB // STRIP) + h
            for j in range(WAYS):
                piece = value[h * STRIP : (h + 1) * STRIP, j * COLS : (j + 1) * COLS]
                m["tv"][p, pl.ds(j * GROUPS, GROUPS)] = piece.reshape(
                    GROUPS, SLICE, COLS
                ).astype(jnp.bfloat16)
    for p in range(REPL):
        m["tv"][p, SHARDS] = edge.astype(jnp.bfloat16)

    pl.semaphore_wait(barrier, 2 + REPL - 1 + TENSORS - 1)
    sent = []

    def replica_exchange(src, dst, sends, recvs, own_sem):
        copies = []
        for d in range(1, REPL):
            peer = wrap(r + d, REPL)
            copies.append(remote(src(peer), dst, sends.at[d], recvs.at[d], {"replica": peer}))
        for copy in copies:
            copy.start()
        own = pltpu.make_async_copy(src(r), dst, own_sem)
        own.start()
        sent.extend(copies)

        def arrive():
            own.wait()
            for copy in copies:
                copy.wait_recv()

        return arrive

    def shard_exchange(src, dst, sends, recvs, own_sem):
        copies = []
        for d in FAR:
            peer = wrap(z + d, SHARDS)
            copies.append(remote(src.at[peer], dst, sends.at[d], recvs.at[d], {"shard": peer}))
        for copy in copies:
            copy.start()
        own = pltpu.make_async_copy(src.at[z], dst, own_sem)
        own.start()
        sent.extend(copies)

        def arrive():
            own.wait()
            for copy in copies:
                copy.wait_recv()

        return arrive

    e1_arrive = replica_exchange(
        lambda p: m["tv"].at[p], m["e1"].at[r], sem["e1_s"], sem["e1_r"], local.at[3]
    )
    rs_copies = []
    for d in range(1, REPL):
        peer = wrap(r + d, REPL)
        rs_copies.append(
            remote(
                grads.at[:, pl.ds(pl.multiple_of(peer * STRIP, STRIP), STRIP), :],
                m["partial"].at[d],
                sem["rs_s"].at[d],
                sem["rs_r"].at[d],
                {"replica": peer},
            )
        )
    for copy in rs_copies:
        copy.start()
    rs_own = pltpu.make_async_copy(
        grads.at[:, pl.ds(pl.multiple_of(r * STRIP, STRIP), STRIP), :],
        m["partial"].at[0],
        local.at[4],
    )
    rs_own.start()
    fl_copies = []
    for d in range(1, TENSORS):
        fl_copies.append(
            remote(
                m["flag"],
                m["flags"].at[d],
                sem["fl_s"].at[d],
                sem["fl_r"].at[d],
                {"tensor": wrap(t + d, TENSORS)},
            )
        )
    for copy in fl_copies:
        copy.start()
    sent += rs_copies + fl_copies

    for _ in range(SHARDS // 2 - 1):
        signal(from_left, {"shard": up})
        signal(from_right, {"shard": down})
        pl.semaphore_wait(from_left, 1)
        pl.semaphore_wait(from_right, 1)
    tab_in.wait()

    e1_arrive()
    for k in range(CAP):
        m["e2"][:, k] = m["e1"][tab[2, REPL + k], 0:SHARDS]
    m["dg"][...] = m["e1"][tab[2, 11], SHARDS]
    e2_arrive = shard_exchange(
        m["e2"], m["mid"].at[z], sem["e2_s"], sem["e2_r"], local.at[5]
    )

    def edge_copy(j):
        return remote(
            m["dg"],
            m["dgs"].at[z],
            sem["dg_s"].at[j],
            sem["dg_r"].at[wrap(z + SHARDS - (r * WAYS + j), SHARDS)],
            {"shard": r * WAYS + j},
        )

    edge_own = pltpu.make_async_copy(m["dg"], m["dgs"].at[z], local.at[6])
    for j in range(WAYS):

        @pl.when(r * WAYS + j != z)
        def _():
            edge_copy(j).start()

        @pl.when(r * WAYS + j == z)
        def _():
            edge_own.start()

    rs_own.wait()
    for copy in rs_copies:
        copy.wait_recv()
    for i in range(SHARED):
        acc = m["partial"][0, i].astype(jnp.float32)
        for d in range(1, REPL):
            acc = acc + m["partial"][d, i].astype(jnp.float32)
        m["summed"][:, i] = acc.reshape(GROUPS, SLICE, COLS).astype(jnp.bfloat16)
    s1_copies = []
    for d in FAR_GROUPS:
        other = wrap(group + d, GROUPS)
        s1_copies.append(
            remote(
                m["summed"].at[other],
                m["spread"].at[group],
                sem["s1_s"].at[d],
                sem["s1_r"].at[d],
                {"shard": other * WAYS + lane},
            )
        )
    for copy in s1_copies:
        copy.start()
    s1_own = pltpu.make_async_copy(
        m["summed"].at[group], m["spread"].at[group], local.at[7]
    )
    s1_own.start()
    sent += s1_copies

    def piece_copy(i):
        to_lane, to_replica = i % WAYS, home_replica(i)
        source = wrap(lane + WAYS - to_lane, WAYS) * REPL + wrap(r + REPL - to_replica, REPL)
        return remote(
            m["summed"].at[:, i],
            m["gin"].at[r, lane],
            sem["gg_s"].at[i],
            sem["gg_r"].at[source],
            {"shard": group * WAYS + to_lane, "replica": to_replica},
        )

    for i in range(SHARED):
        mine = (lane == i % WAYS) & (r == home_replica(i))

        @pl.when(jnp.logical_not(mine))
        def _():
            piece_copy(i).start()

    gin_own = pltpu.make_async_copy(
        m["summed"].at[:, my_block], m["gin"].at[r, lane], local.at[8]
    )

    @pl.when(computes)
    def _():
        gin_own.start()

    e2_arrive()
    for home in range(SHARDS):
        for k in range(CAP):
            pos = tab[1, (home // WAYS) * SHARED + home % WAYS + WAYS * k]
            m["e3"][home, k] = m["mid"][pos >> 1, pos & 1]
    e3_arrive = shard_exchange(
        m["e3"], m["e4"].at[:, pl.ds(z, 1)].at[:, 0], sem["e3_s"], sem["e3_r"], local.at[9]
    )

    s1_own.wait()
    for copy in s1_copies:
        copy.wait_recv()
    for p in range(SHARDS * CAP):
        n = tab[0, p]
        m["picked"][p // CAP, p % CAP] = m["spread"][n >> 3, n & 7]
    s2_arrive = shard_exchange(
        m["picked"],
        m["landed"].at[:, pl.ds(z, 1)].at[:, 0],
        sem["s2_s"],
        sem["s2_r"],
        local.at[10],
    )

    @pl.when(r == group)
    def _():
        for d in range(1, SHARDS):
            pltpu.make_async_copy(m["dg"], m["dgs"].at[0], sem["dg_r"].at[d]).wait()
        edge_own.wait()

    for k in range(CAP):
        pos = tab[1, group * SHARED + lane + WAYS * k]
        m["e4"][k, SHARDS] = jnp.where(
            r == group, m["dgs"][pos >> 1].astype(jnp.float32), 0.0
        ).astype(jnp.bfloat16)

    e3_arrive()

    def part_copy(k, to_replica):
        return remote(
            m["e4"].at[k],
            m["tin"].at[r],
            sem["e4_s"].at[k],
            sem["e4_r"].at[wrap(r + REPL - to_replica, REPL)],
            {"replica": to_replica},
        )

    e4_own = pltpu.make_async_copy(m["e4"].at[core], m["tin"].at[r], local.at[11])
    to_homes = [2 * lane, 2 * wrap(lane + 2, 4) + 1]
    for k in range(CAP):

        @pl.when(r != to_homes[k])
        def _():
            part_copy(k, to_homes[k]).start()

        @pl.when(r == to_homes[k])
        def _():
            e4_own.start()

    s2_arrive()
    for w in range(REPL):
        m["packed"][w] = m["landed"][tab[2, w]]
    s4_arrive = replica_exchange(
        lambda p: m["packed"].at[p], m["strips"].at[r], sem["s4_s"], sem["s4_r"], local.at[12]
    )

    def product(left, right, i):
        return jnp.dot(
            left[pl.ds(i * RB, RB), :], right[...], preferred_element_type=jnp.float32
        )

    size = float(BLOCK * BLOCK)

    @pl.when(computes)
    def _():
        for d in range(1, WAYS * REPL):
            pltpu.make_async_copy(
                m["tiles"].at[0, 0], m["gin"].at[0, 0], sem["gg_r"].at[d]
            ).wait()
        gin_own.wait()
        square_sum = jnp.zeros((STRIP, COLS), jnp.float32)
        for p in range(REPL):
            for j in range(WAYS):
                piece = m["gin"][p, j].astype(jnp.float32).reshape(STRIP, COLS)
                square_sum = square_sum + piece * piece
                block[pl.ds(p * STRIP, STRIP), pl.ds(j * COLS, COLS)] = piece.astype(
                    jnp.bfloat16
                )
        energy = total(square_sum)
        block_t[...] = block[...].T
        for i in range(BLOCK // RB):
            gram[0, pl.ds(i * RB, RB), :] = product(block, block_t, i)
            gram[1, pl.ds(i * RB, RB), :] = product(block_t, block, i)

        for d in range(1, REPL):
            pltpu.make_async_copy(m["e1"].at[0], m["tin"].at[0], sem["e4_r"].at[d]).wait()
        e4_own.wait()
        tri, tri_t = m["tri"], m["tri_t"]
        for p in range(REPL):
            for j in range(WAYS):
                piece = m["tin"][p, pl.ds(j * GROUPS, GROUPS)].astype(jnp.float32)
                tri[pl.ds(p * STRIP, STRIP), pl.ds(j * COLS, COLS)] = piece.reshape(
                    STRIP, COLS
                ).astype(jnp.bfloat16)
        tri_t[...] = tri[...].T
        edge = m["tin"][group, SHARDS].astype(jnp.float32)
        edge = jnp.concatenate([edge[q : q + 1] for q in range(WAYS)], axis=1)
        squares = [jnp.zeros((1, 1), jnp.float32)] * 2
        traces = [jnp.zeros((1, 1), jnp.float32)] * 2
        for i in range(BLOCK // RB):
            span = pl.ds(i * RB, RB)
            at_row, at_col = index_grids(i)
            straight = tri[span, :].astype(jnp.float32)
            turned = tri_t[span, :].astype(jnp.float32)
            stats = [
                jnp.where(at_row <= at_col, straight, turned),
                jnp.where(
                    at_row > at_col, straight, jnp.where(at_row == at_col, edge, turned)
                ),
            ]
            for f in range(2):
                value = decay * stats[f] + gram[f, span, :]
                gram[f, span, :] = value
                squares[f] = squares[f] + total(value * value)
                traces[f] = traces[f] + total(jnp.where(at_row == at_col, value, 0.0))
        shift = damping * (energy / BLOCK + epsilon)
        scales = [
            1.0 / jnp.sqrt(squares[f] + 2.0 * shift * traces[f] + BLOCK * (shift * shift))
            for f in range(2)
        ]
        coup, low1, low2, quart, raw = (
            m["coup"],
            m["low1"],
            m["low2"],
            m["quart"],
            m["raw"],
        )
        for i in range(BLOCK // RB):
            span = pl.ds(i * RB, RB)
            at_row, at_col = index_grids(i)
            eye = at_row == at_col
            for f in range(2):
                coupled = (gram[f, span, :] + jnp.where(eye, shift, 0.0)) * scales[f]
                coup[f, span, :] = coupled.astype(jnp.bfloat16)
                stepper = (jnp.where(eye, 5.0, 0.0) - coupled) * 0.25
                low1[f, span, :] = stepper.astype(jnp.bfloat16)
        for src, dst in ((low1, low2), (low2, quart)):
            for i in range(BLOCK // RB):
                for f in range(2):
                    dst[f, pl.ds(i * RB, RB), :] = product(
                        src.at[f], src.at[f], i
                    ).astype(jnp.bfloat16)
        for i in range(BLOCK // RB):
            at_row, at_col = index_grids(i)
            for f in range(2):
                coupled = product(quart.at[f], coup.at[f], i)
                stepper = (jnp.where(at_row == at_col, 5.0, 0.0) - coupled) * 0.25
                low2[f, pl.ds(i * RB, RB), :] = stepper.astype(jnp.bfloat16)
        for i in range(BLOCK // RB):
            for f in range(2):
                quart[f, pl.ds(i * RB, RB), :] = product(low1.at[f], low2.at[f], i).astype(
                    jnp.bfloat16
                )
        for i in range(BLOCK // RB):
            coup[0, pl.ds(i * RB, RB), :] = product(quart.at[0], block, i).astype(
                jnp.bfloat16
            )
        raw_sum = jnp.zeros((1, 1), jnp.float32)
        for i in range(BLOCK // RB):
            value = product(coup.at[0], quart.at[1], i)
            raw[pl.ds(i * RB, RB), :] = value
            raw_sum = raw_sum + total(value * value)
        graft = jnp.sqrt((energy / size + epsilon) / (raw_sum / size + epsilon))
        for p in range(REPL):
            for j in range(WAYS):
                piece = raw[pl.ds(p * STRIP, STRIP), pl.ds(j * COLS, COLS)] * graft
                m["tiles"][p, j] = piece.reshape(GROUPS, SLICE, COLS).astype(jnp.bfloat16)

    def update_copy(dj, dp):
        to_lane, to_replica = wrap(lane + dj, WAYS), wrap(r + dp, REPL)
        return remote(
            m["tiles"].at[to_replica, to_lane],
            m["final"].at[my_block],
            sem["us_s"].at[dj * REPL + dp],
            sem["us_r"].at[my_block],
            {"shard": group * WAYS + to_lane, "replica": to_replica},
        )

    up_own = pltpu.make_async_copy(
        m["tiles"].at[r, lane], m["final"].at[my_block], local.at[13]
    )

    @pl.when(computes)
    def _():
        for dj in (2, 1, 3, 0):
            for dp in range(REPL):
                if dj or dp:
                    update_copy(dj, dp).start()
        up_own.start()

    s4_arrive()
    holds = tab[2, 10] > 0
    for q in range(REPL):
        strip = m["strips"][q].astype(jnp.float32).reshape(GROUPS, WAYS, SLICE, COLS)
        for j in range(WAYS):
            piece = jnp.where(holds, strip[:, j].reshape(STRIP, COLS), 0.0)
            block[pl.ds(q * STRIP, STRIP), pl.ds(j * COLS, COLS)] = piece.astype(jnp.bfloat16)
    block_t[...] = block[...].T
    trace = jnp.zeros((1, 1), jnp.float32)
    for i in range(BLOCK // RB):
        span = pl.ds(i * RB, RB)
        at_row, at_col = index_grids(i)
        value = decay * stat[0, span, :].astype(jnp.float32) + product(block, block_t, i)
        left_next[span, :] = value.astype(jnp.bfloat16)
        trace = trace + total(jnp.where(at_row == at_col, value, 0.0))
        value = decay * stat[1, span, :].astype(jnp.float32) + product(block_t, block, i)
        right_next[span, :] = value.astype(jnp.bfloat16)
    rms[...] = jnp.broadcast_to(jnp.sqrt(trace / (BLOCK * BLOCK)), rms.shape)

    for copy in fl_copies:
        copy.wait_recv()
    agreed = m["flag"][...]
    for d in range(1, TENSORS):
        agreed = jnp.minimum(agreed, m["flags"][d])
    ok[...] = agreed

    for i in range(SHARED):
        mine = (lane == i % WAYS) & (r == home_replica(i))

        @pl.when(jnp.logical_not(mine))
        def _():
            pltpu.make_async_copy(m["tiles"].at[0, 0], m["final"].at[i], sem["us_r"].at[i]).wait()

    @pl.when(computes)
    def _():
        up_own.wait()

    for i in range(SHARED):
        piece = m["final"][i].astype(jnp.float32).reshape(STRIP, COLS)
        update[i] = piece.astype(jnp.bfloat16)

    for copy in sent:
        copy.wait_send()
    for j in range(WAYS):

        @pl.when(r * WAYS + j != z)
        def _():
            edge_copy(j).wait_send()

    for i in range(SHARED):
        mine = (lane == i % WAYS) & (r == home_replica(i))

        @pl.when(jnp.logical_not(mine))
        def _():
            piece_copy(i).wait_send()

    for k in range(CAP):

        @pl.when(r != to_homes[k])
        def _():
            part_copy(k, to_homes[k]).wait_send()

    @pl.when(computes)
    def _():
        for dj in range(WAYS):
            for dp in range(REPL):
                if dj or dp:
                    update_copy(dj, dp).wait_send()


def balanced_path(block_owner, grads, left_stat, right_stat):
    any_space = pl.BlockSpec(memory_space=pl.ANY)
    vmem = pl.BlockSpec(memory_space=VMEM)
    square = (BLOCK, BLOCK)
    return pl.pallas_call(
        step_kernel,
        out_shape=(
            jax.ShapeDtypeStruct((SHARED, STRIP, COLS), jnp.bfloat16),
            jax.ShapeDtypeStruct((8, 128), jnp.float32),
            jax.ShapeDtypeStruct(square, jnp.bfloat16),
            jax.ShapeDtypeStruct(square, jnp.bfloat16),
            jax.ShapeDtypeStruct((8, 128), jnp.int32),
        ),
        in_specs=[pl.BlockSpec(memory_space=pltpu.SMEM)] + [any_space] * 3,
        out_specs=(vmem,) * 5,
        scratch_shapes=[VMEM(shape, kind) for shape, kind in SCRATCH.values()]
        + [DMA((size,)) for size in SEMS.values()]
        + [
            pltpu.SMEM((8, 128), jnp.int32),
            pltpu.SemaphoreType.REGULAR,
            pltpu.SemaphoreType.REGULAR,
        ],
        compiler_params=pltpu.CompilerParams(
            collective_id=0, has_side_effects=True, vmem_limit_bytes=44 << 20
        ),
    )(block_owner, grads, left_stat, right_stat)


def per_device(grad_parts, block_owner, left_stat, right_stat):
    square = (BLOCK, BLOCK)
    update, rms, left_next, right_next, ok = balanced_path(
        block_owner,
        grad_parts.reshape(SHARED, BLOCK, COLS),
        left_stat.reshape(square),
        right_stat.reshape(square),
    )
    state_shape = (1, 1, 1, 1, BLOCK, BLOCK)
    found = (
        update.reshape(LAYERS, OBT, STRIP, COLS),
        rms[:1, :1].reshape(1, 1, 1, 1),
        left_next.reshape(state_shape),
        right_next.reshape(state_shape),
    )
    return lax.cond(
        ok[0, 0] > 0,
        lambda *_: found,
        general_path,
        grad_parts,
        block_owner,
        left_stat,
        right_stat,
    )


def solution(mesh):
    return jax.shard_map(
        per_device,
        mesh=mesh,
        in_specs=(
            P("replica", None, "tensor", None, "shard"),
            P(None, "tensor", None),
            P("tensor", "shard", None, "replica", None, None),
            P("tensor", "shard", None, "replica", None, None),
        ),
        out_specs=(
            P(None, "tensor", "replica", "shard"),
            P("tensor", "shard", None, "replica"),
            P("tensor", "shard", None, "replica", None, None),
            P("tensor", "shard", None, "replica", None, None),
        ),
        check_vma=False,
    )
```

```python
import jax
import jax.numpy as jnp
from jax import lax
from jax.experimental import pallas as pl
from jax.experimental.pallas import tpu as pltpu
from jax.sharding import PartitionSpec as P

LAYERS = 2
OBT = 4
ITERS = 2


damping = 0.1
epsilon = 1e-06
decay = 0.9


def split_up(shard, dim, length):
    before, after = (shard.shape[:dim], shard.shape[dim + 1 :])
    return jnp.moveaxis(shard.reshape(*before, length, -1, *after), dim, 0)


def summed_on_arrival(shard, axis, dim):
    parts = split_up(shard, dim, lax.axis_size(axis))
    arrived = lax.all_to_all(parts, axis, split_axis=0, concat_axis=0, tiled=True)
    return arrived.astype(jnp.float32).sum(axis=0)


def batched(first_op, second_op, pattern):
    return jnp.einsum(pattern, first_op, second_op, preferred_element_type=jnp.float32)


def inverse_root(factor, energy, extent):
    identity = jnp.eye(extent, dtype=jnp.float32)
    shifted = factor + (damping * (energy / extent + epsilon))[:, None, None] * identity
    scaling = jnp.sqrt(jnp.sum(shifted * shifted, axis=(1, 2), keepdims=True))
    coupled = shifted / scaling
    estimate = coupled
    for sweep in range(ITERS):
        stepper = (5.0 * identity - coupled) / 4.0
        stepper_low = stepper.astype(jnp.bfloat16)
        if sweep == 0:
            estimate = stepper
        else:
            estimate = batched(estimate.astype(jnp.bfloat16), stepper_low, "sij,sjk->sik")
        if sweep + 1 < ITERS:
            squared = batched(stepper_low, stepper_low, "sij,sjk->sik").astype(jnp.bfloat16)
            quartic = batched(squared, squared, "sij,sjk->sik").astype(jnp.bfloat16)
            coupled = batched(quartic, coupled.astype(jnp.bfloat16), "sij,sjk->sik")
    return estimate.astype(jnp.bfloat16)


def precondition(blocks, left_prev, right_prev):
    extent = blocks.shape[-1]
    left_gram = decay * left_prev.astype(jnp.float32) + batched(blocks, blocks, "sij,skj->sik")
    right_gram = decay * right_prev.astype(jnp.float32) + batched(blocks, blocks, "sji,sjk->sik")
    energy = jnp.sum(jnp.square(blocks.astype(jnp.float32)), axis=(1, 2))
    left_root = inverse_root(left_gram, energy, extent)
    right_root = inverse_root(right_gram, energy, extent)
    half_step = batched(left_root, blocks, "sij,sjk->sik").astype(jnp.bfloat16)
    raw_update = batched(half_step, right_root, "sij,sjk->sik")
    mean_grad = energy / (extent * extent)
    mean_raw = jnp.mean(raw_update * raw_update, axis=(1, 2))
    graft_scale = jnp.sqrt((mean_grad + epsilon) / (mean_raw + epsilon))
    result = (raw_update * graft_scale[:, None, None]).astype(jnp.bfloat16)
    left_trace = jnp.sum(jnp.diagonal(left_gram, axis1=1, axis2=2), axis=1)
    stat_rms = jnp.sqrt(left_trace / (extent * extent))
    return (result, stat_rms, left_gram.astype(jnp.bfloat16), right_gram.astype(jnp.bfloat16))


def routing(block_owner, shards, per_shard, capacity, my_shard, ways):
    shared = block_owner.shape[0] * block_owner.shape[1]
    columns = block_owner.shape[2]
    flat_owner = block_owner.reshape(shared, columns)
    dest_shard = flat_owner // per_shard
    order_ids = jnp.arange(shared)
    earlier = order_ids[:, None] < order_ids[None, :]
    same_dest = dest_shard[:, None, :] == dest_shard[None, :, :]
    send_rank = jnp.sum((same_dest & earlier[:, :, None]).astype(jnp.int32), axis=0)
    column_hit = jnp.arange(columns) == my_shard // ways
    my_dest = jnp.sum(jnp.where(column_hit[None, :], dest_shard, 0), axis=1)
    my_rank = jnp.sum(jnp.where(column_hit[None, :], send_rank, 0), axis=1)
    shard_ids = jnp.arange(shards)
    cap_ids = jnp.arange(capacity)
    select_send = (my_dest[None, None, :] == shard_ids[:, None, None]) & (
        my_rank[None, None, :] == cap_ids[None, :, None]
    )
    select_send = select_send.reshape(shards * capacity, shared).astype(jnp.bfloat16)
    slot_ids = my_shard * per_shard + jnp.arange(per_shard)
    slot_match = (flat_owner[None, :, :] == slot_ids[:, None, None]).astype(jnp.float32)
    side_table = (
        shard_ids[None, None, :]
        == ways * jnp.arange(columns)[:, None, None] + jnp.arange(ways)[None, :, None]
    ).astype(jnp.float32)
    rank_table = (send_rank[:, :, None] == cap_ids[None, None, :]).astype(jnp.float32)
    chooser = jnp.einsum("umb,bhs,mbc->uhsc", slot_match, side_table, rank_table)
    chooser = chooser.reshape(per_shard * ways, shards * capacity).astype(jnp.bfloat16)
    return (select_send, chooser)


def general_path(grad_parts, block_owner, left_stat, right_stat):
    replicas = lax.axis_size("replica")
    shards = lax.axis_size("shard")
    my_shard = lax.axis_index("shard")
    extent = grad_parts.shape[3]
    part_cols = grad_parts.shape[4]
    ways = extent // part_cols
    strip_rows = extent // replicas
    shared = LAYERS * OBT
    capacity = (shared + shards - 1) // shards
    slot_count = (shared // ways + replicas - 1) // replicas
    per_shard = slot_count * replicas
    piece_size = strip_rows * part_cols
    grouped = grad_parts.reshape(LAYERS, OBT, replicas, strip_rows, part_cols)
    summed = summed_on_arrival(grouped, "replica", 2)
    pieces = summed.astype(jnp.bfloat16).reshape(shared, piece_size)
    select_send, chooser = routing(block_owner, shards, per_shard, capacity, my_shard, ways)
    outgoing = jnp.dot(select_send, pieces, preferred_element_type=jnp.float32).astype(jnp.bfloat16)
    outgoing = outgoing.reshape(shards, capacity, strip_rows, part_cols)
    arrived = lax.all_to_all(outgoing, "shard", split_axis=0, concat_axis=0, tiled=True)
    gathered = jnp.dot(
        chooser, arrived.reshape(shards * capacity, piece_size), preferred_element_type=jnp.float32
    ).astype(jnp.bfloat16)
    gathered = gathered.reshape(per_shard, ways, strip_rows, part_cols).transpose(0, 2, 1, 3)
    gathered = gathered.reshape(slot_count, replicas, strip_rows, extent)
    blocks = lax.all_to_all(gathered, "replica", split_axis=1, concat_axis=1, tiled=True).reshape(
        slot_count, extent, extent
    )
    left_prev = left_stat.reshape(slot_count, extent, extent)
    right_prev = right_stat.reshape(slot_count, extent, extent)
    updated, block_norms, left_next, right_next = precondition(blocks, left_prev, right_prev)
    spread = lax.all_to_all(
        updated.reshape(slot_count, replicas, strip_rows, extent),
        "replica",
        split_axis=1,
        concat_axis=1,
        tiled=True,
    )
    spread = (
        spread.reshape(per_shard, strip_rows, ways, part_cols)
        .transpose(0, 2, 1, 3)
        .reshape(per_shard * ways, piece_size)
    )
    outgoing_back = jnp.dot(chooser.T, spread, preferred_element_type=jnp.float32).astype(
        jnp.bfloat16
    )
    outgoing_back = outgoing_back.reshape(shards, capacity, strip_rows, part_cols)
    returned = lax.all_to_all(outgoing_back, "shard", split_axis=0, concat_axis=0, tiled=True)
    mine = jnp.dot(
        select_send.T,
        returned.reshape(shards * capacity, piece_size),
        preferred_element_type=jnp.float32,
    ).astype(jnp.bfloat16)
    state_shape = (1, 1, slot_count, 1, extent, extent)
    return (
        mine.reshape(LAYERS, OBT, strip_rows, part_cols),
        block_norms.reshape(1, 1, slot_count, 1),
        left_next.reshape(state_shape),
        right_next.reshape(state_shape),
    )


BLOCK = 512
SHARDS = 32
REPL = 8
TENSORS = 4
WAYS = 4
GROUPS = 8
SHARED = 8
CAP = 2
STRIP = 64
COLS = 128
SLICE = 8
RB = 128
MESH = pl.DeviceIdType.MESH
VMEM = pltpu.VMEM
DMA = pltpu.SemaphoreType.DMA
FAR = [16] + [d for k in range(15, 0, -1) for d in (k, SHARDS - k)]
FAR_GROUPS = [3, 4, 2, 5, 1, 6, 0, 7]
REACH = 8
TURN = 2
SCRATCH = dict(
    tab_v=((8, 128), jnp.int32),
    flag=((8, 128), jnp.int32),
    flags=((TENSORS, 8, 128), jnp.int32),
    stat=((2, BLOCK, BLOCK), jnp.bfloat16),
    tv=((REPL, SHARDS + 1, SLICE, COLS), jnp.bfloat16),
    e1=((REPL, SHARDS + 1, SLICE, COLS), jnp.bfloat16),
    e2=((SHARDS, CAP, SLICE, COLS), jnp.bfloat16),
    dg=((SLICE, COLS), jnp.bfloat16),
    mid=((SHARDS, CAP, SLICE, COLS), jnp.bfloat16),
    dgs=((SHARDS, SLICE, COLS), jnp.bfloat16),
    e3=((SHARDS, CAP, SLICE, COLS), jnp.bfloat16),
    e3in=((SHARDS, CAP, SLICE, COLS), jnp.bfloat16),
    e4=((CAP, SHARDS + 1, SLICE, COLS), jnp.bfloat16),
    tin=((REPL, SHARDS + 1, SLICE, COLS), jnp.bfloat16),
    partial=((REPL, SHARED, STRIP, COLS), jnp.bfloat16),
    summed=((GROUPS, SHARED, SLICE, COLS), jnp.bfloat16),
    spread=((GROUPS, SHARED, SLICE, COLS), jnp.bfloat16),
    picked=((SHARDS, CAP, SLICE, COLS), jnp.bfloat16),
    landed=((SHARDS, CAP, SLICE, COLS), jnp.bfloat16),
    packed=((REPL, SHARDS, SLICE, COLS), jnp.bfloat16),
    strips=((REPL, SHARDS, SLICE, COLS), jnp.bfloat16),
    gin=((REPL, WAYS, GROUPS, SLICE, COLS), jnp.bfloat16),
    block=((BLOCK, BLOCK), jnp.bfloat16),
    block_t=((BLOCK, BLOCK), jnp.bfloat16),
    tri=((BLOCK, BLOCK), jnp.bfloat16),
    tri_t=((BLOCK, BLOCK), jnp.bfloat16),
    gram=((2, BLOCK, BLOCK), jnp.float32),
    coup=((2, BLOCK, BLOCK), jnp.bfloat16),
    low1=((2, BLOCK, BLOCK), jnp.bfloat16),
    low2=((2, BLOCK, BLOCK), jnp.bfloat16),
    quart=((2, BLOCK, BLOCK), jnp.bfloat16),
    raw=((BLOCK, BLOCK), jnp.float32),
    tiles=((REPL, WAYS, GROUPS, SLICE, COLS), jnp.bfloat16),
    final=((SHARED, GROUPS, SLICE, COLS), jnp.bfloat16),
)
SEMS = dict(
    local=16,
    fl_s=TENSORS,
    fl_r=TENSORS,
    e1_s=REPL,
    e1_r=REPL,
    e2_s=SHARDS,
    e2_r=SHARDS,
    dg_s=WAYS,
    dg_r=SHARDS,
    e3_s=SHARDS,
    e3_r=SHARDS,
    e4_s=CAP,
    e4_r=REPL,
    rs_s=REPL,
    rs_r=REPL,
    s1_s=GROUPS,
    s1_r=GROUPS,
    s2_s=SHARDS,
    s2_r=SHARDS,
    s4_s=REPL,
    s4_r=REPL,
    gg_s=SHARED,
    gg_r=WAYS * REPL,
    us_s=WAYS * REPL,
    us_r=SHARED,
)


def wrap(value, extent):
    return lax.rem(value, extent)


def total(value):
    return jnp.sum(value, axis=(0, 1), keepdims=True)


def index_grids(i):
    rows = lax.broadcasted_iota(jnp.int32, (RB, BLOCK), 0) + i * RB
    return rows, lax.broadcasted_iota(jnp.int32, (RB, BLOCK), 1)


def home_replica(i):
    core = i // WAYS
    return 2 * ((i % WAYS + 2 * core) % 4) + core


def step_kernel(owner, grads, left_stat, right_stat, update, rms, left_next, right_next, ok, *rest):
    names = list(SCRATCH)
    m = dict(zip(names, rest[: len(names)]))
    rest = rest[len(names) :]
    sem = dict(zip(SEMS, rest[: len(SEMS)]))
    tab, from_left, from_right = rest[len(SEMS) :]
    stat, block, block_t, gram = m["stat"], m["block"], m["block_t"], m["gram"]
    local = sem["local"]

    t = lax.axis_index("tensor")
    z = lax.axis_index("shard")
    r = lax.axis_index("replica")
    group = z // WAYS
    lane = wrap(z, WAYS)
    core = wrap(r, 2)
    computes = r // 2 == wrap(lane + 2 * core, 4)
    my_block = lane + WAYS * core

    stat_in = [
        pltpu.make_async_copy(left_stat, stat.at[0], local.at[0]),
        pltpu.make_async_copy(right_stat, stat.at[1], local.at[1]),
    ]
    for copy in stat_in:
        copy.start()

    def remote(src, dst, send, recv, where):
        return pltpu.make_async_remote_copy(
            src_ref=src,
            dst_ref=dst,
            send_sem=send,
            recv_sem=recv,
            device_id=where,
            device_id_type=MESH,
        )

    def signal(semaphore, where):
        pl.semaphore_signal(semaphore, inc=1, device_id=where, device_id_type=MESH)

    barrier = pltpu.get_barrier_semaphore()
    for d in range(REACH, 0, -1):
        signal(barrier, {"shard": wrap(z + d, SHARDS)})
        signal(barrier, {"shard": wrap(z + SHARDS - d, SHARDS)})
    for d in range(1, REPL):
        signal(barrier, {"replica": wrap(r + d, REPL)})
    for d in range(1, TENSORS):
        signal(barrier, {"tensor": wrap(t + d, TENSORS)})

    lanes = lax.broadcasted_iota(jnp.int32, (1, 128), 1)
    rows8 = lax.broadcasted_iota(jnp.int32, (SHARED, 128), 0)
    across = jnp.full((1, 128), -8, jnp.int32)
    columns = []
    for b in range(GROUPS):
        column = jnp.zeros((SHARED, 128), jnp.int32)
        for i in range(SHARED):
            value = owner[i // OBT, i % OBT, b]
            across = jnp.where(lanes == b * SHARED + i, value, across)
            column = jnp.where(rows8 == i, value, column)
        columns.append(column)
    down_w = jnp.concatenate(columns, axis=0)
    count = GROUPS * SHARED
    n_down = lax.broadcasted_iota(jnp.int32, (count, 128), 0)
    n_across = lax.broadcasted_iota(jnp.int32, (count, 128), 1)
    dest_down = down_w >> 3
    same = dest_down == (across >> 3)
    rank_across = jnp.sum(
        jnp.where(same & (n_down < n_across), 1, 0), axis=0, keepdims=True
    )
    rank_down = jnp.sum(jnp.where(same & (n_across < n_down), 1, 0), axis=1, keepdims=True)
    most = jnp.max(rank_down, axis=0, keepdims=True)
    m["flag"][...] = jnp.broadcast_to(jnp.where(most < CAP, 1, 0), (8, 128))
    rank_across = jnp.minimum(rank_across, CAP - 1)
    rank_down = jnp.minimum(rank_down, CAP - 1)
    place_down = dest_down * CAP + rank_down
    inverse = jnp.sum(jnp.where(place_down == n_across, n_down, 0), axis=0, keepdims=True)
    pick = jnp.where(
        n_across < REPL,
        jnp.where(down_w == z * REPL + n_across, rank_down, 0),
        jnp.where(
            n_across < REPL + CAP,
            jnp.where(place_down == z * CAP + n_across - REPL, down_w & 7, 0),
            jnp.where(
                n_across == 10,
                jnp.where(down_w == z * REPL + r, 1, 0),
                jnp.where((dest_down == z) & ((n_down >> 3) == r), down_w & 7, 0),
            ),
        ),
    )
    pick = jnp.sum(pick, axis=0, keepdims=True)
    m["tab_v"][0:1, :] = jnp.minimum(inverse, count - 1)
    m["tab_v"][1:2, :] = jnp.clip((across >> 3) * CAP + rank_across, 0, count - 1)
    m["tab_v"][2:3, :] = jnp.minimum(pick, jnp.where(lanes < REPL, CAP - 1, REPL - 1))
    m["tab_v"][3:8, :] = jnp.zeros((5, 128), jnp.int32)
    tab_in = pltpu.make_async_copy(m["tab_v"], tab, local.at[2])
    tab_in.start()

    for copy in stat_in:
        copy.wait()
    rows8 = lax.broadcasted_iota(jnp.int32, (SLICE, COLS), 0)
    eye = lax.broadcasted_iota(jnp.int32, (COLS, COLS), 0) == lax.broadcasted_iota(
        jnp.int32, (COLS, COLS), 1
    )
    edge = jnp.zeros((SLICE, COLS), jnp.float32)
    for q in range(WAYS):
        span = pl.ds(q * COLS, COLS)
        value = jnp.where(eye, stat[1, span, span].astype(jnp.float32), 0.0)
        edge = jnp.where(rows8 == q, jnp.sum(value, axis=0, keepdims=True), edge)
    for i in range(BLOCK // RB):
        span = pl.ds(i * RB, RB)
        at_row, at_col = index_grids(i)
        value = jnp.where(
            at_row <= at_col,
            stat[0, span, :].astype(jnp.float32),
            stat[1, span, :].astype(jnp.float32),
        )
        for h in range(RB // STRIP):
            p = i * (RB // STRIP) + h
            for j in range(WAYS):
                piece = value[h * STRIP : (h + 1) * STRIP, j * COLS : (j + 1) * COLS]
                m["tv"][p, pl.ds(j * GROUPS, GROUPS)] = piece.reshape(
                    GROUPS, SLICE, COLS
                ).astype(jnp.bfloat16)
    for p in range(REPL):
        m["tv"][p, SHARDS] = edge.astype(jnp.bfloat16)

    pl.semaphore_wait(barrier, 2 * REACH + REPL - 1 + TENSORS - 1)
    sent = []

    def replica_exchange(src, dst, sends, recvs, own_sem):
        copies = []
        for d in range(1, REPL):
            peer = wrap(r + d, REPL)
            copies.append(remote(src(peer), dst, sends.at[d], recvs.at[d], {"replica": peer}))
        for copy in copies:
            copy.start()
        own = pltpu.make_async_copy(src(r), dst, own_sem)
        own.start()
        sent.extend(copies)

        def arrive():
            own.wait()
            for copy in copies:
                copy.wait_recv()

        return arrive

    def shard_exchange(src, dst, sends, recvs, own_sem):
        copies = []
        for d in FAR:
            peer = wrap(z + d, SHARDS)
            copies.append(remote(src.at[peer], dst, sends.at[d], recvs.at[d], {"shard": peer}))
        for copy in copies:
            copy.start()
        own = pltpu.make_async_copy(src.at[z], dst, own_sem)
        own.start()
        sent.extend(copies)

        def arrive():
            own.wait()
            for copy in copies:
                copy.wait_recv()

        return arrive

    e1_arrive = replica_exchange(
        lambda p: m["tv"].at[p], m["e1"].at[r], sem["e1_s"], sem["e1_r"], local.at[3]
    )
    rs_copies = []
    for d in range(1, REPL):
        peer = wrap(r + d, REPL)
        rs_copies.append(
            remote(
                grads.at[:, pl.ds(pl.multiple_of(peer * STRIP, STRIP), STRIP), :],
                m["partial"].at[d],
                sem["rs_s"].at[d],
                sem["rs_r"].at[d],
                {"replica": peer},
            )
        )
    for copy in rs_copies:
        copy.start()
    rs_own = pltpu.make_async_copy(
        grads.at[:, pl.ds(pl.multiple_of(r * STRIP, STRIP), STRIP), :],
        m["partial"].at[0],
        local.at[4],
    )
    rs_own.start()
    fl_copies = []
    for d in range(1, TENSORS):
        fl_copies.append(
            remote(
                m["flag"],
                m["flags"].at[d],
                sem["fl_s"].at[d],
                sem["fl_r"].at[d],
                {"tensor": wrap(t + d, TENSORS)},
            )
        )
    for copy in fl_copies:
        copy.start()
    sent += rs_copies + fl_copies

    signal(from_left, {"shard": wrap(z + REACH, SHARDS)})
    signal(from_right, {"shard": wrap(z + SHARDS - REACH, SHARDS)})
    pl.semaphore_wait(from_left, 1)
    pl.semaphore_wait(from_right, 1)
    tab_in.wait()

    e1_arrive()
    for k in range(CAP):
        m["e2"][:, k] = m["e1"][tab[2, REPL + k], 0:SHARDS]
    m["dg"][...] = m["e1"][tab[2, 11], SHARDS]
    e2_arrive = shard_exchange(
        m["e2"], m["mid"].at[z], sem["e2_s"], sem["e2_r"], local.at[5]
    )

    def edge_copy(j):
        return remote(
            m["dg"],
            m["dgs"].at[z],
            sem["dg_s"].at[j],
            sem["dg_r"].at[wrap(z + SHARDS - (r * WAYS + j), SHARDS)],
            {"shard": r * WAYS + j},
        )

    edge_own = pltpu.make_async_copy(m["dg"], m["dgs"].at[z], local.at[6])
    for j in range(WAYS):

        @pl.when(r * WAYS + j != z)
        def _():
            edge_copy(j).start()

        @pl.when(r * WAYS + j == z)
        def _():
            edge_own.start()

    rs_own.wait()
    for copy in rs_copies:
        copy.wait_recv()
    for i in range(SHARED):
        acc = m["partial"][0, i].astype(jnp.float32)
        for d in range(1, REPL):
            acc = acc + m["partial"][d, i].astype(jnp.float32)
        m["summed"][:, i] = acc.reshape(GROUPS, SLICE, COLS).astype(jnp.bfloat16)
    s1_copies = []
    for d in FAR_GROUPS:
        other = wrap(group + d, GROUPS)
        s1_copies.append(
            remote(
                m["summed"].at[other],
                m["spread"].at[group],
                sem["s1_s"].at[d],
                sem["s1_r"].at[d],
                {"shard": wrap(other * WAYS + lane + TURN, SHARDS)},
            )
        )
    for copy in s1_copies:
        copy.start()
    sent += s1_copies

    def piece_copy(i):
        to_lane, to_replica = i % WAYS, home_replica(i)
        source = wrap(lane + WAYS - to_lane, WAYS) * REPL + wrap(r + REPL - to_replica, REPL)
        return remote(
            m["summed"].at[:, i],
            m["gin"].at[r, lane],
            sem["gg_s"].at[i],
            sem["gg_r"].at[source],
            {"shard": group * WAYS + to_lane, "replica": to_replica},
        )

    for i in range(SHARED):
        mine = (lane == i % WAYS) & (r == home_replica(i))

        @pl.when(jnp.logical_not(mine))
        def _():
            piece_copy(i).start()

    gin_own = pltpu.make_async_copy(
        m["summed"].at[:, my_block], m["gin"].at[r, lane], local.at[8]
    )

    @pl.when(computes)
    def _():
        gin_own.start()

    e2_arrive()
    for home in range(SHARDS):
        for k in range(CAP):
            pos = tab[1, (home // WAYS) * SHARED + home % WAYS + WAYS * k]
            m["e3"][home, k] = m["mid"][pos >> 1, pos & 1]
    e3_arrive = shard_exchange(
        m["e3"], m["e3in"].at[z], sem["e3_s"], sem["e3_r"], local.at[9]
    )

    for copy in s1_copies:
        copy.wait_recv()
    for p in range(SHARDS * CAP):
        n = tab[0, p]
        m["picked"][p // CAP, p % CAP] = m["spread"][n >> 3, n & 7]
    s2_arrive = shard_exchange(
        m["picked"],
        m["landed"].at[wrap(z + SHARDS - TURN, SHARDS)],
        sem["s2_s"],
        sem["s2_r"],
        local.at[10],
    )

    @pl.when(r == group)
    def _():
        for d in range(1, SHARDS):
            pltpu.make_async_copy(m["dg"], m["dgs"].at[0], sem["dg_r"].at[d]).wait()
        edge_own.wait()

    for k in range(CAP):
        pos = tab[1, group * SHARED + lane + WAYS * k]
        m["e4"][k, SHARDS] = jnp.where(
            r == group, m["dgs"][pos >> 1].astype(jnp.float32), 0.0
        ).astype(jnp.bfloat16)

    e3_arrive()
    for k in range(CAP):
        m["e4"][k, 0:SHARDS] = m["e3in"][:, k]

    def part_copy(k, to_replica):
        return remote(
            m["e4"].at[k],
            m["tin"].at[r],
            sem["e4_s"].at[k],
            sem["e4_r"].at[wrap(r + REPL - to_replica, REPL)],
            {"replica": to_replica},
        )

    e4_own = pltpu.make_async_copy(m["e4"].at[core], m["tin"].at[r], local.at[11])
    to_homes = [2 * lane, 2 * wrap(lane + 2, 4) + 1]
    for k in range(CAP):

        @pl.when(r != to_homes[k])
        def _():
            part_copy(k, to_homes[k]).start()

        @pl.when(r == to_homes[k])
        def _():
            e4_own.start()

    def product(left, right, i):
        return jnp.dot(
            left[pl.ds(i * RB, RB), :], right[...], preferred_element_type=jnp.float32
        )

    size = float(BLOCK * BLOCK)

    @pl.when(computes)
    def _():
        for d in range(1, WAYS * REPL):
            pltpu.make_async_copy(
                m["tiles"].at[0, 0], m["gin"].at[0, 0], sem["gg_r"].at[d]
            ).wait()
        gin_own.wait()
        square_sum = jnp.zeros((STRIP, COLS), jnp.float32)
        for p in range(REPL):
            for j in range(WAYS):
                piece = m["gin"][p, j].astype(jnp.float32).reshape(STRIP, COLS)
                square_sum = square_sum + piece * piece
                block[pl.ds(p * STRIP, STRIP), pl.ds(j * COLS, COLS)] = piece.astype(
                    jnp.bfloat16
                )
        energy = total(square_sum)
        block_t[...] = block[...].T
        for i in range(BLOCK // RB):
            gram[0, pl.ds(i * RB, RB), :] = product(block, block_t, i)
            gram[1, pl.ds(i * RB, RB), :] = product(block_t, block, i)

        for d in range(1, REPL):
            pltpu.make_async_copy(m["e1"].at[0], m["tin"].at[0], sem["e4_r"].at[d]).wait()
        e4_own.wait()
        tri, tri_t = m["tri"], m["tri_t"]
        for p in range(REPL):
            for j in range(WAYS):
                piece = m["tin"][p, pl.ds(j * GROUPS, GROUPS)].astype(jnp.float32)
                tri[pl.ds(p * STRIP, STRIP), pl.ds(j * COLS, COLS)] = piece.reshape(
                    STRIP, COLS
                ).astype(jnp.bfloat16)
        tri_t[...] = tri[...].T
        edge = m["tin"][group, SHARDS].astype(jnp.float32)
        edge = jnp.concatenate([edge[q : q + 1] for q in range(WAYS)], axis=1)
        squares = [jnp.zeros((1, 1), jnp.float32)] * 2
        traces = [jnp.zeros((1, 1), jnp.float32)] * 2
        for i in range(BLOCK // RB):
            span = pl.ds(i * RB, RB)
            at_row, at_col = index_grids(i)
            straight = tri[span, :].astype(jnp.float32)
            turned = tri_t[span, :].astype(jnp.float32)
            stats = [
                jnp.where(at_row <= at_col, straight, turned),
                jnp.where(
                    at_row > at_col, straight, jnp.where(at_row == at_col, edge, turned)
                ),
            ]
            for f in range(2):
                value = decay * stats[f] + gram[f, span, :]
                gram[f, span, :] = value
                squares[f] = squares[f] + total(value * value)
                traces[f] = traces[f] + total(jnp.where(at_row == at_col, value, 0.0))
        shift = damping * (energy / BLOCK + epsilon)
        scales = [
            1.0 / jnp.sqrt(squares[f] + 2.0 * shift * traces[f] + BLOCK * (shift * shift))
            for f in range(2)
        ]
        coup, low1, low2, quart, raw = (
            m["coup"],
            m["low1"],
            m["low2"],
            m["quart"],
            m["raw"],
        )
        for i in range(BLOCK // RB):
            span = pl.ds(i * RB, RB)
            at_row, at_col = index_grids(i)
            eye = at_row == at_col
            for f in range(2):
                coupled = (gram[f, span, :] + jnp.where(eye, shift, 0.0)) * scales[f]
                coup[f, span, :] = coupled.astype(jnp.bfloat16)
                stepper = (jnp.where(eye, 5.0, 0.0) - coupled) * 0.25
                low1[f, span, :] = stepper.astype(jnp.bfloat16)
        for src, dst in ((low1, low2), (low2, quart)):
            for i in range(BLOCK // RB):
                for f in range(2):
                    dst[f, pl.ds(i * RB, RB), :] = product(
                        src.at[f], src.at[f], i
                    ).astype(jnp.bfloat16)
        for i in range(BLOCK // RB):
            at_row, at_col = index_grids(i)
            for f in range(2):
                coupled = product(quart.at[f], coup.at[f], i)
                stepper = (jnp.where(at_row == at_col, 5.0, 0.0) - coupled) * 0.25
                low2[f, pl.ds(i * RB, RB), :] = stepper.astype(jnp.bfloat16)
        for i in range(BLOCK // RB):
            for f in range(2):
                quart[f, pl.ds(i * RB, RB), :] = product(low1.at[f], low2.at[f], i).astype(
                    jnp.bfloat16
                )
        for i in range(BLOCK // RB):
            coup[0, pl.ds(i * RB, RB), :] = product(quart.at[0], block, i).astype(
                jnp.bfloat16
            )
        raw_sum = jnp.zeros((1, 1), jnp.float32)
        for i in range(BLOCK // RB):
            value = product(coup.at[0], quart.at[1], i)
            raw[pl.ds(i * RB, RB), :] = value
            raw_sum = raw_sum + total(value * value)
        graft = jnp.sqrt((energy / size + epsilon) / (raw_sum / size + epsilon))
        for p in range(REPL):
            for j in range(WAYS):
                piece = raw[pl.ds(p * STRIP, STRIP), pl.ds(j * COLS, COLS)] * graft
                m["tiles"][p, j] = piece.reshape(GROUPS, SLICE, COLS).astype(jnp.bfloat16)

    def update_copy(dj, dp):
        to_lane, to_replica = wrap(lane + dj, WAYS), wrap(r + dp, REPL)
        return remote(
            m["tiles"].at[to_replica, to_lane],
            m["final"].at[my_block],
            sem["us_s"].at[dj * REPL + dp],
            sem["us_r"].at[my_block],
            {"shard": group * WAYS + to_lane, "replica": to_replica},
        )

    up_own = pltpu.make_async_copy(
        m["tiles"].at[r, lane], m["final"].at[my_block], local.at[13]
    )

    @pl.when(computes)
    def _():
        for dj in (2, 1, 3, 0):
            for dp in range(REPL):
                if dj or dp:
                    update_copy(dj, dp).start()
        up_own.start()

    s2_arrive()
    for w in range(REPL):
        m["packed"][w] = m["landed"][:, tab[2, w]]
    s4_arrive = replica_exchange(
        lambda p: m["packed"].at[p], m["strips"].at[r], sem["s4_s"], sem["s4_r"], local.at[12]
    )

    s4_arrive()
    holds = tab[2, 10] > 0
    for q in range(REPL):
        strip = m["strips"][q].astype(jnp.float32).reshape(GROUPS, WAYS, SLICE, COLS)
        for j in range(WAYS):
            piece = jnp.where(holds, strip[:, j].reshape(STRIP, COLS), 0.0)
            block[pl.ds(q * STRIP, STRIP), pl.ds(j * COLS, COLS)] = piece.astype(jnp.bfloat16)
    block_t[...] = block[...].T
    trace = jnp.zeros((1, 1), jnp.float32)
    for i in range(BLOCK // RB):
        span = pl.ds(i * RB, RB)
        at_row, at_col = index_grids(i)
        value = decay * stat[0, span, :].astype(jnp.float32) + product(block, block_t, i)
        left_next[span, :] = value.astype(jnp.bfloat16)
        trace = trace + total(jnp.where(at_row == at_col, value, 0.0))
        value = decay * stat[1, span, :].astype(jnp.float32) + product(block_t, block, i)
        right_next[span, :] = value.astype(jnp.bfloat16)
    rms[...] = jnp.broadcast_to(jnp.sqrt(trace / (BLOCK * BLOCK)), rms.shape)

    for copy in fl_copies:
        copy.wait_recv()
    agreed = m["flag"][...]
    for d in range(1, TENSORS):
        agreed = jnp.minimum(agreed, m["flags"][d])
    ok[0, 0] = jnp.min(agreed)

    for i in range(SHARED):
        mine = (lane == i % WAYS) & (r == home_replica(i))

        @pl.when(jnp.logical_not(mine))
        def _():
            pltpu.make_async_copy(m["tiles"].at[0, 0], m["final"].at[i], sem["us_r"].at[i]).wait()

    @pl.when(computes)
    def _():
        up_own.wait()

    for i in range(SHARED):
        piece = m["final"][i].astype(jnp.float32).reshape(STRIP, COLS)
        update[i] = piece.astype(jnp.bfloat16)

    for copy in sent:
        copy.wait_send()
    for j in range(WAYS):

        @pl.when(r * WAYS + j != z)
        def _():
            edge_copy(j).wait_send()

    for i in range(SHARED):
        mine = (lane == i % WAYS) & (r == home_replica(i))

        @pl.when(jnp.logical_not(mine))
        def _():
            piece_copy(i).wait_send()

    for k in range(CAP):

        @pl.when(r != to_homes[k])
        def _():
            part_copy(k, to_homes[k]).wait_send()

    @pl.when(computes)
    def _():
        for dj in range(WAYS):
            for dp in range(REPL):
                if dj or dp:
                    update_copy(dj, dp).wait_send()


def balanced_path(block_owner, grads, left_stat, right_stat):
    any_space = pl.BlockSpec(memory_space=pl.ANY)
    vmem = pl.BlockSpec(memory_space=VMEM)
    square = (BLOCK, BLOCK)
    return pl.pallas_call(
        step_kernel,
        out_shape=(
            jax.ShapeDtypeStruct((SHARED, STRIP, COLS), jnp.bfloat16),
            jax.ShapeDtypeStruct((8, 128), jnp.float32),
            jax.ShapeDtypeStruct(square, jnp.bfloat16),
            jax.ShapeDtypeStruct(square, jnp.bfloat16),
            jax.ShapeDtypeStruct((1, 1), jnp.int32),
        ),
        in_specs=[pl.BlockSpec(memory_space=pltpu.SMEM)] + [any_space] * 3,
        out_specs=(vmem,) * 4 + (pl.BlockSpec(memory_space=pltpu.SMEM),),
        scratch_shapes=[VMEM(shape, kind) for shape, kind in SCRATCH.values()]
        + [DMA((size,)) for size in SEMS.values()]
        + [
            pltpu.SMEM((8, 128), jnp.int32),
            pltpu.SemaphoreType.REGULAR,
            pltpu.SemaphoreType.REGULAR,
        ],
        compiler_params=pltpu.CompilerParams(
            collective_id=0, has_side_effects=True, vmem_limit_bytes=44 << 20
        ),
    )(block_owner, grads, left_stat, right_stat)


def per_device(grad_parts, block_owner, left_stat, right_stat):
    square = (BLOCK, BLOCK)
    update, rms, left_next, right_next, ok = balanced_path(
        block_owner,
        grad_parts.reshape(SHARED, BLOCK, COLS),
        left_stat.reshape(square),
        right_stat.reshape(square),
    )
    state_shape = (1, 1, 1, 1, BLOCK, BLOCK)
    found = (
        update.reshape(LAYERS, OBT, STRIP, COLS),
        rms[:1, :1].reshape(1, 1, 1, 1),
        left_next.reshape(state_shape),
        right_next.reshape(state_shape),
    )
    return lax.cond(
        ok[0, 0] > 0,
        lambda *_: found,
        general_path,
        grad_parts,
        block_owner,
        left_stat,
        right_stat,
    )


def solution(mesh):
    return jax.shard_map(
        per_device,
        mesh=mesh,
        in_specs=(
            P("replica", None, "tensor", None, "shard"),
            P(None, "tensor", None),
            P("tensor", "shard", None, "replica", None, None),
            P("tensor", "shard", None, "replica", None, None),
        ),
        out_specs=(
            P(None, "tensor", "replica", "shard"),
            P("tensor", "shard", None, "replica"),
            P("tensor", "shard", None, "replica", None, None),
            P("tensor", "shard", None, "replica", None, None),
        ),
        check_vma=False,
    )
```

```python
import jax
import jax.numpy as jnp
from jax import lax
from jax.experimental import pallas as pl
from jax.experimental.pallas import tpu as pltpu
from jax.sharding import PartitionSpec as P

LAYERS = 2
OBT = 4
ITERS = 2


damping = 0.1
epsilon = 1e-06
decay = 0.9


def split_up(shard, dim, length):
    before, after = (shard.shape[:dim], shard.shape[dim + 1 :])
    return jnp.moveaxis(shard.reshape(*before, length, -1, *after), dim, 0)


def summed_on_arrival(shard, axis, dim):
    parts = split_up(shard, dim, lax.axis_size(axis))
    arrived = lax.all_to_all(parts, axis, split_axis=0, concat_axis=0, tiled=True)
    return arrived.astype(jnp.float32).sum(axis=0)


def batched(first_op, second_op, pattern):
    return jnp.einsum(pattern, first_op, second_op, preferred_element_type=jnp.float32)


def inverse_root(factor, energy, extent):
    identity = jnp.eye(extent, dtype=jnp.float32)
    shifted = factor + (damping * (energy / extent + epsilon))[:, None, None] * identity
    scaling = jnp.sqrt(jnp.sum(shifted * shifted, axis=(1, 2), keepdims=True))
    coupled = shifted / scaling
    estimate = coupled
    for sweep in range(ITERS):
        stepper = (5.0 * identity - coupled) / 4.0
        stepper_low = stepper.astype(jnp.bfloat16)
        if sweep == 0:
            estimate = stepper
        else:
            estimate = batched(estimate.astype(jnp.bfloat16), stepper_low, "sij,sjk->sik")
        if sweep + 1 < ITERS:
            squared = batched(stepper_low, stepper_low, "sij,sjk->sik").astype(jnp.bfloat16)
            quartic = batched(squared, squared, "sij,sjk->sik").astype(jnp.bfloat16)
            coupled = batched(quartic, coupled.astype(jnp.bfloat16), "sij,sjk->sik")
    return estimate.astype(jnp.bfloat16)


def precondition(blocks, left_prev, right_prev):
    extent = blocks.shape[-1]
    left_gram = decay * left_prev.astype(jnp.float32) + batched(blocks, blocks, "sij,skj->sik")
    right_gram = decay * right_prev.astype(jnp.float32) + batched(blocks, blocks, "sji,sjk->sik")
    energy = jnp.sum(jnp.square(blocks.astype(jnp.float32)), axis=(1, 2))
    left_root = inverse_root(left_gram, energy, extent)
    right_root = inverse_root(right_gram, energy, extent)
    half_step = batched(left_root, blocks, "sij,sjk->sik").astype(jnp.bfloat16)
    raw_update = batched(half_step, right_root, "sij,sjk->sik")
    mean_grad = energy / (extent * extent)
    mean_raw = jnp.mean(raw_update * raw_update, axis=(1, 2))
    graft_scale = jnp.sqrt((mean_grad + epsilon) / (mean_raw + epsilon))
    result = (raw_update * graft_scale[:, None, None]).astype(jnp.bfloat16)
    left_trace = jnp.sum(jnp.diagonal(left_gram, axis1=1, axis2=2), axis=1)
    stat_rms = jnp.sqrt(left_trace / (extent * extent))
    return (result, stat_rms, left_gram.astype(jnp.bfloat16), right_gram.astype(jnp.bfloat16))


def routing(block_owner, shards, per_shard, capacity, my_shard, ways):
    shared = block_owner.shape[0] * block_owner.shape[1]
    columns = block_owner.shape[2]
    flat_owner = block_owner.reshape(shared, columns)
    dest_shard = flat_owner // per_shard
    order_ids = jnp.arange(shared)
    earlier = order_ids[:, None] < order_ids[None, :]
    same_dest = dest_shard[:, None, :] == dest_shard[None, :, :]
    send_rank = jnp.sum((same_dest & earlier[:, :, None]).astype(jnp.int32), axis=0)
    column_hit = jnp.arange(columns) == my_shard // ways
    my_dest = jnp.sum(jnp.where(column_hit[None, :], dest_shard, 0), axis=1)
    my_rank = jnp.sum(jnp.where(column_hit[None, :], send_rank, 0), axis=1)
    shard_ids = jnp.arange(shards)
    cap_ids = jnp.arange(capacity)
    select_send = (my_dest[None, None, :] == shard_ids[:, None, None]) & (
        my_rank[None, None, :] == cap_ids[None, :, None]
    )
    select_send = select_send.reshape(shards * capacity, shared).astype(jnp.bfloat16)
    slot_ids = my_shard * per_shard + jnp.arange(per_shard)
    slot_match = (flat_owner[None, :, :] == slot_ids[:, None, None]).astype(jnp.float32)
    side_table = (
        shard_ids[None, None, :]
        == ways * jnp.arange(columns)[:, None, None] + jnp.arange(ways)[None, :, None]
    ).astype(jnp.float32)
    rank_table = (send_rank[:, :, None] == cap_ids[None, None, :]).astype(jnp.float32)
    chooser = jnp.einsum("umb,bhs,mbc->uhsc", slot_match, side_table, rank_table)
    chooser = chooser.reshape(per_shard * ways, shards * capacity).astype(jnp.bfloat16)
    return (select_send, chooser)


def general_path(grad_parts, block_owner, left_stat, right_stat):
    replicas = lax.axis_size("replica")
    shards = lax.axis_size("shard")
    my_shard = lax.axis_index("shard")
    extent = grad_parts.shape[3]
    part_cols = grad_parts.shape[4]
    ways = extent // part_cols
    strip_rows = extent // replicas
    shared = LAYERS * OBT
    capacity = (shared + shards - 1) // shards
    slot_count = (shared // ways + replicas - 1) // replicas
    per_shard = slot_count * replicas
    piece_size = strip_rows * part_cols
    grouped = grad_parts.reshape(LAYERS, OBT, replicas, strip_rows, part_cols)
    summed = summed_on_arrival(grouped, "replica", 2)
    pieces = summed.astype(jnp.bfloat16).reshape(shared, piece_size)
    select_send, chooser = routing(block_owner, shards, per_shard, capacity, my_shard, ways)
    outgoing = jnp.dot(select_send, pieces, preferred_element_type=jnp.float32).astype(jnp.bfloat16)
    outgoing = outgoing.reshape(shards, capacity, strip_rows, part_cols)
    arrived = lax.all_to_all(outgoing, "shard", split_axis=0, concat_axis=0, tiled=True)
    gathered = jnp.dot(
        chooser, arrived.reshape(shards * capacity, piece_size), preferred_element_type=jnp.float32
    ).astype(jnp.bfloat16)
    gathered = gathered.reshape(per_shard, ways, strip_rows, part_cols).transpose(0, 2, 1, 3)
    gathered = gathered.reshape(slot_count, replicas, strip_rows, extent)
    blocks = lax.all_to_all(gathered, "replica", split_axis=1, concat_axis=1, tiled=True).reshape(
        slot_count, extent, extent
    )
    left_prev = left_stat.reshape(slot_count, extent, extent)
    right_prev = right_stat.reshape(slot_count, extent, extent)
    updated, block_norms, left_next, right_next = precondition(blocks, left_prev, right_prev)
    spread = lax.all_to_all(
        updated.reshape(slot_count, replicas, strip_rows, extent),
        "replica",
        split_axis=1,
        concat_axis=1,
        tiled=True,
    )
    spread = (
        spread.reshape(per_shard, strip_rows, ways, part_cols)
        .transpose(0, 2, 1, 3)
        .reshape(per_shard * ways, piece_size)
    )
    outgoing_back = jnp.dot(chooser.T, spread, preferred_element_type=jnp.float32).astype(
        jnp.bfloat16
    )
    outgoing_back = outgoing_back.reshape(shards, capacity, strip_rows, part_cols)
    returned = lax.all_to_all(outgoing_back, "shard", split_axis=0, concat_axis=0, tiled=True)
    mine = jnp.dot(
        select_send.T,
        returned.reshape(shards * capacity, piece_size),
        preferred_element_type=jnp.float32,
    ).astype(jnp.bfloat16)
    state_shape = (1, 1, slot_count, 1, extent, extent)
    return (
        mine.reshape(LAYERS, OBT, strip_rows, part_cols),
        block_norms.reshape(1, 1, slot_count, 1),
        left_next.reshape(state_shape),
        right_next.reshape(state_shape),
    )


BLOCK = 512
SHARDS = 32
REPL = 8
TENSORS = 4
WAYS = 4
GROUPS = 8
SHARED = 8
CAP = 2
STRIP = 64
COLS = 128
SLICE = 8
RB = 128
MESH = pl.DeviceIdType.MESH
VMEM = pltpu.VMEM
DMA = pltpu.SemaphoreType.DMA
FAR = [16] + [d for k in range(15, 0, -1) for d in (k, SHARDS - k)]
FAR_GROUPS = [3, 4, 2, 5, 1, 6, 0, 7]
REACH = 8
TURN = 2
SCRATCH = dict(
    tab_v=((8, 128), jnp.int32),
    flag=((8, 128), jnp.int32),
    flags=((TENSORS, 8, 128), jnp.int32),
    stat=((2, BLOCK, BLOCK), jnp.bfloat16),
    tv=((REPL, SHARDS + 1, SLICE, COLS), jnp.bfloat16),
    e1=((REPL, SHARDS + 1, SLICE, COLS), jnp.bfloat16),
    e2=((SHARDS, CAP, SLICE, COLS), jnp.bfloat16),
    dg=((SLICE, COLS), jnp.bfloat16),
    mid=((SHARDS, CAP, SLICE, COLS), jnp.bfloat16),
    dgs=((SHARDS, SLICE, COLS), jnp.bfloat16),
    e3=((SHARDS, CAP, SLICE, COLS), jnp.bfloat16),
    e3in=((SHARDS, CAP, SLICE, COLS), jnp.bfloat16),
    e4=((CAP, SHARDS + 1, SLICE, COLS), jnp.bfloat16),
    tin=((REPL, SHARDS + 1, SLICE, COLS), jnp.bfloat16),
    partial=((REPL, SHARED, STRIP, COLS), jnp.bfloat16),
    summed=((GROUPS, SHARED, SLICE, COLS), jnp.bfloat16),
    spread=((GROUPS, SHARED, SLICE, COLS), jnp.bfloat16),
    picked=((SHARDS, CAP, SLICE, COLS), jnp.bfloat16),
    landed=((SHARDS, CAP, SLICE, COLS), jnp.bfloat16),
    packed=((REPL, SHARDS, SLICE, COLS), jnp.bfloat16),
    strips=((REPL, SHARDS, SLICE, COLS), jnp.bfloat16),
    gin=((REPL, WAYS, GROUPS, SLICE, COLS), jnp.bfloat16),
    block=((BLOCK, BLOCK), jnp.bfloat16),
    block_t=((BLOCK, BLOCK), jnp.bfloat16),
    tri=((BLOCK, BLOCK), jnp.bfloat16),
    tri_t=((BLOCK, BLOCK), jnp.bfloat16),
    gram=((2, BLOCK, BLOCK), jnp.float32),
    coup=((2, BLOCK, BLOCK), jnp.bfloat16),
    low1=((2, BLOCK, BLOCK), jnp.bfloat16),
    low2=((2, BLOCK, BLOCK), jnp.bfloat16),
    quart=((2, BLOCK, BLOCK), jnp.bfloat16),
    raw=((BLOCK, BLOCK), jnp.float32),
    tiles=((REPL, WAYS, GROUPS, SLICE, COLS), jnp.bfloat16),
    final=((SHARED, GROUPS, SLICE, COLS), jnp.bfloat16),
)
SEMS = dict(
    local=16,
    fl_s=TENSORS,
    fl_r=TENSORS,
    e1_s=REPL,
    e1_r=REPL,
    e2_s=SHARDS,
    e2_r=SHARDS,
    dg_s=WAYS,
    dg_r=SHARDS,
    e3_s=SHARDS,
    e3_r=SHARDS,
    e4_s=CAP,
    e4_r=REPL,
    rs_s=REPL,
    rs_r=REPL,
    s1_s=GROUPS,
    s1_r=GROUPS,
    s2_s=SHARDS,
    s2_r=SHARDS,
    s4_s=REPL,
    s4_r=REPL,
    gg_s=SHARED,
    gg_r=WAYS * REPL,
    us_s=WAYS * REPL,
    us_r=SHARED,
)


def wrap(value, extent):
    return lax.rem(value, extent)


def total(value):
    return jnp.sum(value, axis=(0, 1), keepdims=True)


def index_grids(i):
    rows = lax.broadcasted_iota(jnp.int32, (RB, BLOCK), 0) + i * RB
    return rows, lax.broadcasted_iota(jnp.int32, (RB, BLOCK), 1)


def home_replica(i):
    core = i // WAYS
    return 2 * ((i % WAYS + 2 * core) % 4) + core


def step_kernel(owner, grads, left_stat, right_stat, update, rms, left_next, right_next, ok, *rest):
    names = list(SCRATCH)
    m = dict(zip(names, rest[: len(names)]))
    rest = rest[len(names) :]
    sem = dict(zip(SEMS, rest[: len(SEMS)]))
    tab, from_left, from_right = rest[len(SEMS) :]
    stat, block, block_t, gram = m["stat"], m["block"], m["block_t"], m["gram"]
    local = sem["local"]

    t = lax.axis_index("tensor")
    z = lax.axis_index("shard")
    r = lax.axis_index("replica")
    group = z // WAYS
    lane = wrap(z, WAYS)
    core = wrap(r, 2)
    computes = r // 2 == wrap(lane + 2 * core, 4)
    my_block = lane + WAYS * core

    stat_in = [
        pltpu.make_async_copy(left_stat, stat.at[0], local.at[0]),
        pltpu.make_async_copy(right_stat, stat.at[1], local.at[1]),
    ]
    for copy in stat_in:
        copy.start()

    def remote(src, dst, send, recv, where):
        return pltpu.make_async_remote_copy(
            src_ref=src,
            dst_ref=dst,
            send_sem=send,
            recv_sem=recv,
            device_id=where,
            device_id_type=MESH,
        )

    def signal(semaphore, where):
        pl.semaphore_signal(semaphore, inc=1, device_id=where, device_id_type=MESH)

    barrier = pltpu.get_barrier_semaphore()
    for d in range(REACH, 0, -1):
        signal(barrier, {"shard": wrap(z + d, SHARDS)})
        signal(barrier, {"shard": wrap(z + SHARDS - d, SHARDS)})
    for d in range(1, REPL):
        signal(barrier, {"replica": wrap(r + d, REPL)})
    for d in range(1, TENSORS):
        signal(barrier, {"tensor": wrap(t + d, TENSORS)})

    lanes = lax.broadcasted_iota(jnp.int32, (1, 128), 1)
    rows8 = lax.broadcasted_iota(jnp.int32, (SHARED, 128), 0)
    across = jnp.full((1, 128), -8, jnp.int32)
    columns = []
    for b in range(GROUPS):
        column = jnp.zeros((SHARED, 128), jnp.int32)
        for i in range(SHARED):
            value = owner[i // OBT, i % OBT, b]
            across = jnp.where(lanes == b * SHARED + i, value, across)
            column = jnp.where(rows8 == i, value, column)
        columns.append(column)
    down_w = jnp.concatenate(columns, axis=0)
    count = GROUPS * SHARED
    n_down = lax.broadcasted_iota(jnp.int32, (count, 128), 0)
    n_across = lax.broadcasted_iota(jnp.int32, (count, 128), 1)
    dest_down = down_w >> 3
    same = dest_down == (across >> 3)
    rank_across = jnp.sum(
        jnp.where(same & (n_down < n_across), 1, 0), axis=0, keepdims=True
    )
    rank_down = jnp.sum(jnp.where(same & (n_across < n_down), 1, 0), axis=1, keepdims=True)
    most = jnp.max(rank_down, axis=0, keepdims=True)
    m["flag"][...] = jnp.broadcast_to(jnp.where(most < CAP, 1, 0), (8, 128))
    rank_across = jnp.minimum(rank_across, CAP - 1)
    rank_down = jnp.minimum(rank_down, CAP - 1)
    place_down = dest_down * CAP + rank_down
    inverse = jnp.sum(jnp.where(place_down == n_across, n_down, 0), axis=0, keepdims=True)
    pick = jnp.where(
        n_across < REPL,
        jnp.where(down_w == z * REPL + n_across, rank_down, 0),
        jnp.where(
            n_across < REPL + CAP,
            jnp.where(place_down == z * CAP + n_across - REPL, down_w & 7, 0),
            jnp.where(
                n_across == 10,
                jnp.where(down_w == z * REPL + r, 1, 0),
                jnp.where((dest_down == z) & ((n_down >> 3) == r), down_w & 7, 0),
            ),
        ),
    )
    pick = jnp.sum(pick, axis=0, keepdims=True)
    m["tab_v"][0:1, :] = jnp.minimum(inverse, count - 1)
    m["tab_v"][1:2, :] = jnp.clip((across >> 3) * CAP + rank_across, 0, count - 1)
    m["tab_v"][2:3, :] = jnp.minimum(pick, jnp.where(lanes < REPL, CAP - 1, REPL - 1))
    m["tab_v"][3:8, :] = jnp.zeros((5, 128), jnp.int32)
    tab_in = pltpu.make_async_copy(m["tab_v"], tab, local.at[2])
    tab_in.start()

    for copy in stat_in:
        copy.wait()
    rows8 = lax.broadcasted_iota(jnp.int32, (SLICE, COLS), 0)
    eye = lax.broadcasted_iota(jnp.int32, (COLS, COLS), 0) == lax.broadcasted_iota(
        jnp.int32, (COLS, COLS), 1
    )
    edge = jnp.zeros((SLICE, COLS), jnp.float32)
    for q in range(WAYS):
        span = pl.ds(q * COLS, COLS)
        value = jnp.where(eye, stat[1, span, span].astype(jnp.float32), 0.0)
        edge = jnp.where(rows8 == q, jnp.sum(value, axis=0, keepdims=True), edge)
    for i in range(BLOCK // RB):
        span = pl.ds(i * RB, RB)
        at_row, at_col = index_grids(i)
        value = jnp.where(
            at_row <= at_col,
            stat[0, span, :].astype(jnp.float32),
            stat[1, span, :].astype(jnp.float32),
        )
        for h in range(RB // STRIP):
            p = i * (RB // STRIP) + h
            for j in range(WAYS):
                piece = value[h * STRIP : (h + 1) * STRIP, j * COLS : (j + 1) * COLS]
                m["tv"][p, pl.ds(j * GROUPS, GROUPS)] = piece.reshape(
                    GROUPS, SLICE, COLS
                ).astype(jnp.bfloat16)
    for p in range(REPL):
        m["tv"][p, SHARDS] = edge.astype(jnp.bfloat16)

    pl.semaphore_wait(barrier, 2 * REACH + REPL - 1 + TENSORS - 1)
    sent = []

    def replica_exchange(src, dst, sends, recvs, own_sem):
        copies = []
        for d in range(1, REPL):
            peer = wrap(r + d, REPL)
            copies.append(remote(src(peer), dst, sends.at[d], recvs.at[d], {"replica": peer}))
        for copy in copies:
            copy.start()
        own = pltpu.make_async_copy(src(r), dst, own_sem)
        own.start()
        sent.extend(copies)

        def arrive():
            own.wait()
            for copy in copies:
                copy.wait_recv()

        return arrive

    def shard_exchange(src, dst, sends, recvs, own_sem):
        copies = []
        for d in FAR:
            peer = wrap(z + d, SHARDS)
            copies.append(remote(src.at[peer], dst, sends.at[d], recvs.at[d], {"shard": peer}))
        for copy in copies:
            copy.start()
        own = pltpu.make_async_copy(src.at[z], dst, own_sem)
        own.start()
        sent.extend(copies)

        def arrive():
            own.wait()
            for copy in copies:
                copy.wait_recv()

        return arrive

    e1_arrive = replica_exchange(
        lambda p: m["tv"].at[p], m["e1"].at[r], sem["e1_s"], sem["e1_r"], local.at[3]
    )
    rs_copies = []
    for d in range(1, REPL):
        peer = wrap(r + d, REPL)
        rs_copies.append(
            remote(
                grads.at[:, pl.ds(pl.multiple_of(peer * STRIP, STRIP), STRIP), :],
                m["partial"].at[d],
                sem["rs_s"].at[d],
                sem["rs_r"].at[d],
                {"replica": peer},
            )
        )
    for copy in rs_copies:
        copy.start()
    rs_own = pltpu.make_async_copy(
        grads.at[:, pl.ds(pl.multiple_of(r * STRIP, STRIP), STRIP), :],
        m["partial"].at[0],
        local.at[4],
    )
    rs_own.start()
    fl_copies = []
    for d in range(1, TENSORS):
        fl_copies.append(
            remote(
                m["flag"],
                m["flags"].at[d],
                sem["fl_s"].at[d],
                sem["fl_r"].at[d],
                {"tensor": wrap(t + d, TENSORS)},
            )
        )
    for copy in fl_copies:
        copy.start()
    sent += rs_copies + fl_copies

    signal(from_left, {"shard": wrap(z + REACH, SHARDS)})
    signal(from_right, {"shard": wrap(z + SHARDS - REACH, SHARDS)})
    pl.semaphore_wait(from_left, 1)
    pl.semaphore_wait(from_right, 1)
    tab_in.wait()

    e1_arrive()
    for k in range(CAP):
        m["e2"][:, k] = m["e1"][tab[2, REPL + k], 0:SHARDS]
    m["dg"][...] = m["e1"][tab[2, 11], SHARDS]
    e2_arrive = shard_exchange(
        m["e2"], m["mid"].at[z], sem["e2_s"], sem["e2_r"], local.at[5]
    )

    def edge_copy(j):
        return remote(
            m["dg"],
            m["dgs"].at[z],
            sem["dg_s"].at[j],
            sem["dg_r"].at[wrap(z + SHARDS - (r * WAYS + j), SHARDS)],
            {"shard": r * WAYS + j},
        )

    edge_own = pltpu.make_async_copy(m["dg"], m["dgs"].at[z], local.at[6])
    for j in range(WAYS):

        @pl.when(r * WAYS + j != z)
        def _():
            edge_copy(j).start()

        @pl.when(r * WAYS + j == z)
        def _():
            edge_own.start()

    rs_own.wait()
    for copy in rs_copies:
        copy.wait_recv()
    for i in range(SHARED):
        acc = m["partial"][0, i].astype(jnp.float32)
        for d in range(1, REPL):
            acc = acc + m["partial"][d, i].astype(jnp.float32)
        m["summed"][:, i] = acc.reshape(GROUPS, SLICE, COLS).astype(jnp.bfloat16)
    s1_copies = []
    for d in FAR_GROUPS:
        other = wrap(group + d, GROUPS)
        s1_copies.append(
            remote(
                m["summed"].at[other],
                m["spread"].at[group],
                sem["s1_s"].at[d],
                sem["s1_r"].at[d],
                {"shard": wrap(other * WAYS + lane + TURN, SHARDS)},
            )
        )
    for copy in s1_copies:
        copy.start()
    sent += s1_copies

    def piece_copy(i):
        to_lane, to_replica = i % WAYS, home_replica(i)
        source = wrap(lane + WAYS - to_lane, WAYS) * REPL + wrap(r + REPL - to_replica, REPL)
        return remote(
            m["summed"].at[:, i],
            m["gin"].at[r, lane],
            sem["gg_s"].at[i],
            sem["gg_r"].at[source],
            {"shard": group * WAYS + to_lane, "replica": to_replica},
        )

    for i in range(SHARED):
        mine = (lane == i % WAYS) & (r == home_replica(i))

        @pl.when(jnp.logical_not(mine))
        def _():
            piece_copy(i).start()

    gin_own = pltpu.make_async_copy(
        m["summed"].at[:, my_block], m["gin"].at[r, lane], local.at[8]
    )

    @pl.when(computes)
    def _():
        gin_own.start()

    e2_arrive()
    for home in range(SHARDS):
        for k in range(CAP):
            pos = tab[1, (home // WAYS) * SHARED + home % WAYS + WAYS * k]
            m["e3"][home, k] = m["mid"][pos >> 1, pos & 1]
    e3_arrive = shard_exchange(
        m["e3"], m["e3in"].at[z], sem["e3_s"], sem["e3_r"], local.at[9]
    )

    for copy in s1_copies:
        copy.wait_recv()
    for p in range(SHARDS * CAP):
        n = tab[0, p]
        m["picked"][p // CAP, p % CAP] = m["spread"][n >> 3, n & 7]
    s2_arrive = shard_exchange(
        m["picked"],
        m["landed"].at[wrap(z + SHARDS - TURN, SHARDS)],
        sem["s2_s"],
        sem["s2_r"],
        local.at[10],
    )

    @pl.when(r == group)
    def _():
        for d in range(1, SHARDS):
            pltpu.make_async_copy(m["dg"], m["dgs"].at[0], sem["dg_r"].at[d]).wait()
        edge_own.wait()

    for k in range(CAP):
        pos = tab[1, group * SHARED + lane + WAYS * k]
        m["e4"][k, SHARDS] = jnp.where(
            r == group, m["dgs"][pos >> 1].astype(jnp.float32), 0.0
        ).astype(jnp.bfloat16)

    e3_arrive()
    for k in range(CAP):
        m["e4"][k, 0:SHARDS] = m["e3in"][:, k]

    def part_copy(k, to_replica):
        return remote(
            m["e4"].at[k],
            m["tin"].at[r],
            sem["e4_s"].at[k],
            sem["e4_r"].at[wrap(r + REPL - to_replica, REPL)],
            {"replica": to_replica},
        )

    e4_own = pltpu.make_async_copy(m["e4"].at[core], m["tin"].at[r], local.at[11])
    to_homes = [2 * lane, 2 * wrap(lane + 2, 4) + 1]
    for k in range(CAP):

        @pl.when(r != to_homes[k])
        def _():
            part_copy(k, to_homes[k]).start()

        @pl.when(r == to_homes[k])
        def _():
            e4_own.start()

    def product(left, right, i):
        return jnp.dot(
            left[pl.ds(i * RB, RB), :], right[...], preferred_element_type=jnp.float32
        )

    size = float(BLOCK * BLOCK)

    @pl.when(computes)
    def _():
        for d in range(1, WAYS * REPL):
            pltpu.make_async_copy(
                m["tiles"].at[0, 0], m["gin"].at[0, 0], sem["gg_r"].at[d]
            ).wait()
        gin_own.wait()
        square_sum = jnp.zeros((STRIP, COLS), jnp.float32)
        for p in range(REPL):
            for j in range(WAYS):
                piece = m["gin"][p, j].astype(jnp.float32).reshape(STRIP, COLS)
                square_sum = square_sum + piece * piece
                block[pl.ds(p * STRIP, STRIP), pl.ds(j * COLS, COLS)] = piece.astype(
                    jnp.bfloat16
                )
        energy = total(square_sum)
        block_t[...] = block[...].T
        for i in range(BLOCK // RB):
            gram[0, pl.ds(i * RB, RB), :] = product(block, block_t, i)
            gram[1, pl.ds(i * RB, RB), :] = product(block_t, block, i)

        for d in range(1, REPL):
            pltpu.make_async_copy(m["e1"].at[0], m["tin"].at[0], sem["e4_r"].at[d]).wait()
        e4_own.wait()
        tri, tri_t = m["tri"], m["tri_t"]
        for p in range(REPL):
            for j in range(WAYS):
                piece = m["tin"][p, pl.ds(j * GROUPS, GROUPS)].astype(jnp.float32)
                tri[pl.ds(p * STRIP, STRIP), pl.ds(j * COLS, COLS)] = piece.reshape(
                    STRIP, COLS
                ).astype(jnp.bfloat16)
        tri_t[...] = tri[...].T
        edge = m["tin"][group, SHARDS].astype(jnp.float32)
        edge = jnp.concatenate([edge[q : q + 1] for q in range(WAYS)], axis=1)
        squares = [jnp.zeros((1, 1), jnp.float32)] * 2
        traces = [jnp.zeros((1, 1), jnp.float32)] * 2
        for i in range(BLOCK // RB):
            span = pl.ds(i * RB, RB)
            at_row, at_col = index_grids(i)
            straight = tri[span, :].astype(jnp.float32)
            turned = tri_t[span, :].astype(jnp.float32)
            stats = [
                jnp.where(at_row <= at_col, straight, turned),
                jnp.where(
                    at_row > at_col, straight, jnp.where(at_row == at_col, edge, turned)
                ),
            ]
            for f in range(2):
                value = decay * stats[f] + gram[f, span, :]
                gram[f, span, :] = value
                squares[f] = squares[f] + total(value * value)
                traces[f] = traces[f] + total(jnp.where(at_row == at_col, value, 0.0))
        shift = damping * (energy / BLOCK + epsilon)
        scales = [
            1.0 / jnp.sqrt(squares[f] + 2.0 * shift * traces[f] + BLOCK * (shift * shift))
            for f in range(2)
        ]
        coup, low1, low2, quart, raw = (
            m["coup"],
            m["low1"],
            m["low2"],
            m["quart"],
            m["raw"],
        )
        for i in range(BLOCK // RB):
            span = pl.ds(i * RB, RB)
            at_row, at_col = index_grids(i)
            eye = at_row == at_col
            for f in range(2):
                coupled = (gram[f, span, :] + jnp.where(eye, shift, 0.0)) * scales[f]
                coup[f, span, :] = coupled.astype(jnp.bfloat16)
                stepper = (jnp.where(eye, 5.0, 0.0) - coupled) * 0.25
                low1[f, span, :] = stepper.astype(jnp.bfloat16)
        for src, dst in ((low1, low2), (low2, quart)):
            for i in range(BLOCK // RB):
                for f in range(2):
                    dst[f, pl.ds(i * RB, RB), :] = product(
                        src.at[f], src.at[f], i
                    ).astype(jnp.bfloat16)
        for i in range(BLOCK // RB):
            at_row, at_col = index_grids(i)
            for f in range(2):
                coupled = product(quart.at[f], coup.at[f], i)
                stepper = (jnp.where(at_row == at_col, 5.0, 0.0) - coupled) * 0.25
                low2[f, pl.ds(i * RB, RB), :] = stepper.astype(jnp.bfloat16)
        for i in range(BLOCK // RB):
            for f in range(2):
                quart[f, pl.ds(i * RB, RB), :] = product(low1.at[f], low2.at[f], i).astype(
                    jnp.bfloat16
                )
        for i in range(BLOCK // RB):
            coup[0, pl.ds(i * RB, RB), :] = product(quart.at[0], block, i).astype(
                jnp.bfloat16
            )
        raw_sum = jnp.zeros((1, 1), jnp.float32)
        for i in range(BLOCK // RB):
            value = product(coup.at[0], quart.at[1], i)
            raw[pl.ds(i * RB, RB), :] = value
            raw_sum = raw_sum + total(value * value)
        graft = jnp.sqrt((energy / size + epsilon) / (raw_sum / size + epsilon))
        for p in range(REPL):
            for j in range(WAYS):
                piece = raw[pl.ds(p * STRIP, STRIP), pl.ds(j * COLS, COLS)] * graft
                m["tiles"][p, j] = piece.reshape(GROUPS, SLICE, COLS).astype(jnp.bfloat16)

    def update_copy(dj, dp):
        to_lane, to_replica = wrap(lane + dj, WAYS), wrap(r + dp, REPL)
        return remote(
            m["tiles"].at[to_replica, to_lane],
            m["final"].at[my_block],
            sem["us_s"].at[dj * REPL + dp],
            sem["us_r"].at[my_block],
            {"shard": group * WAYS + to_lane, "replica": to_replica},
        )

    up_own = pltpu.make_async_copy(
        m["tiles"].at[r, lane], m["final"].at[my_block], local.at[13]
    )

    @pl.when(computes)
    def _():
        for dj in (2, 1, 3, 0):
            for dp in range(REPL):
                if dj or dp:
                    update_copy(dj, dp).start()
        up_own.start()

    s2_arrive()
    for w in range(REPL):
        m["packed"][w] = m["landed"][:, tab[2, w]]
    s4_arrive = replica_exchange(
        lambda p: m["packed"].at[p], m["strips"].at[r], sem["s4_s"], sem["s4_r"], local.at[12]
    )

    s4_arrive()
    holds = tab[2, 10] > 0
    for q in range(REPL):
        strip = m["strips"][q].astype(jnp.float32).reshape(GROUPS, WAYS, SLICE, COLS)
        for j in range(WAYS):
            piece = jnp.where(holds, strip[:, j].reshape(STRIP, COLS), 0.0)
            block[pl.ds(q * STRIP, STRIP), pl.ds(j * COLS, COLS)] = piece.astype(jnp.bfloat16)
    block_t[...] = block[...].T
    trace = jnp.zeros((1, 1), jnp.float32)
    for i in range(BLOCK // RB):
        span = pl.ds(i * RB, RB)
        at_row, at_col = index_grids(i)
        value = decay * stat[0, span, :].astype(jnp.float32) + product(block, block_t, i)
        left_next[span, :] = value.astype(jnp.bfloat16)
        trace = trace + total(jnp.where(at_row == at_col, value, 0.0))
        value = decay * stat[1, span, :].astype(jnp.float32) + product(block_t, block, i)
        right_next[span, :] = value.astype(jnp.bfloat16)
    rms[...] = jnp.broadcast_to(jnp.sqrt(trace / (BLOCK * BLOCK)), rms.shape)

    for copy in fl_copies:
        copy.wait_recv()
    agreed = m["flag"][...]
    for d in range(1, TENSORS):
        agreed = jnp.minimum(agreed, m["flags"][d])
    ok[0, 0] = jnp.min(agreed)

    for i in range(SHARED):
        mine = (lane == i % WAYS) & (r == home_replica(i))

        @pl.when(jnp.logical_not(mine))
        def _():
            pltpu.make_async_copy(m["tiles"].at[0, 0], m["final"].at[i], sem["us_r"].at[i]).wait()

    @pl.when(computes)
    def _():
        up_own.wait()

    for i in range(SHARED):
        piece = m["final"][i].astype(jnp.float32).reshape(STRIP, COLS)
        update[i] = piece.astype(jnp.bfloat16)

    for copy in sent:
        copy.wait_send()
    for j in range(WAYS):

        @pl.when(r * WAYS + j != z)
        def _():
            edge_copy(j).wait_send()

    for i in range(SHARED):
        mine = (lane == i % WAYS) & (r == home_replica(i))

        @pl.when(jnp.logical_not(mine))
        def _():
            piece_copy(i).wait_send()

    for k in range(CAP):

        @pl.when(r != to_homes[k])
        def _():
            part_copy(k, to_homes[k]).wait_send()

    @pl.when(computes)
    def _():
        for dj in range(WAYS):
            for dp in range(REPL):
                if dj or dp:
                    update_copy(dj, dp).wait_send()


def balanced_path(block_owner, grads, left_stat, right_stat):
    any_space = pl.BlockSpec(memory_space=pl.ANY)
    vmem = pl.BlockSpec(memory_space=VMEM)
    square = (BLOCK, BLOCK)
    return pl.pallas_call(
        step_kernel,
        out_shape=(
            jax.ShapeDtypeStruct((SHARED, STRIP, COLS), jnp.bfloat16),
            jax.ShapeDtypeStruct((8, 128), jnp.float32),
            jax.ShapeDtypeStruct(square, jnp.bfloat16),
            jax.ShapeDtypeStruct(square, jnp.bfloat16),
            jax.ShapeDtypeStruct((1, 1), jnp.int32),
        ),
        in_specs=[pl.BlockSpec(memory_space=pltpu.SMEM)] + [any_space] * 3,
        out_specs=(vmem,) * 4 + (pl.BlockSpec(memory_space=pltpu.SMEM),),
        scratch_shapes=[VMEM(shape, kind) for shape, kind in SCRATCH.values()]
        + [DMA((size,)) for size in SEMS.values()]
        + [
            pltpu.SMEM((8, 128), jnp.int32),
            pltpu.SemaphoreType.REGULAR,
            pltpu.SemaphoreType.REGULAR,
        ],
        compiler_params=pltpu.CompilerParams(
            collective_id=0, has_side_effects=True, vmem_limit_bytes=44 << 20
        ),
    )(block_owner, grads, left_stat, right_stat)


def write_kernel(*refs):
    count = len(refs) // 2
    sources, targets, sems = refs[:count], refs[count : 2 * count], refs[2 * count]
    copies = [
        pltpu.make_async_copy(src, dst, sems.at[k])
        for k, (src, dst) in enumerate(zip(sources, targets))
    ]
    for copy in copies:
        copy.start()
    for copy in copies:
        copy.wait()


def written(*arrays):
    return pl.pallas_call(
        write_kernel,
        out_shape=tuple(jax.ShapeDtypeStruct(a.shape, a.dtype) for a in arrays),
        in_specs=[pl.BlockSpec(memory_space=VMEM)] * len(arrays),
        out_specs=(pl.BlockSpec(memory_space=pltpu.HBM),) * len(arrays),
        scratch_shapes=[DMA((len(arrays),))],
    )(*arrays)


def per_device(grad_parts, block_owner, left_stat, right_stat):
    square = (BLOCK, BLOCK)
    update, rms, left_next, right_next, ok = balanced_path(
        block_owner,
        grad_parts.reshape(SHARED, BLOCK, COLS),
        left_stat.reshape(square),
        right_stat.reshape(square),
    )
    state_shape = (1, 1, 1, 1, BLOCK, BLOCK)

    def finish(update, rms, left_next, right_next, *_):
        update, left_next, right_next = written(update, left_next, right_next)
        return (
            update.reshape(LAYERS, OBT, STRIP, COLS),
            rms[:1, :1].reshape(1, 1, 1, 1),
            left_next.reshape(state_shape),
            right_next.reshape(state_shape),
        )

    return lax.cond(
        ok[0, 0] > 0,
        finish,
        lambda *args: general_path(*args[4:]),
        update,
        rms,
        left_next,
        right_next,
        grad_parts,
        block_owner,
        left_stat,
        right_stat,
    )


def solution(mesh):
    return jax.shard_map(
        per_device,
        mesh=mesh,
        in_specs=(
            P("replica", None, "tensor", None, "shard"),
            P(None, "tensor", None),
            P("tensor", "shard", None, "replica", None, None),
            P("tensor", "shard", None, "replica", None, None),
        ),
        out_specs=(
            P(None, "tensor", "replica", "shard"),
            P("tensor", "shard", None, "replica"),
            P("tensor", "shard", None, "replica", None, None),
            P("tensor", "shard", None, "replica", None, None),
        ),
        check_vma=False,
    )
```
